128 devices in a mesh: xs: 4 (over x), bx: 32 (over z, y, core).
Axes of the slice: x: 4, y: 4, z: 4, core: 2. Of those that a mesh axis runs over, the one named last changes fastest.
Arguments:
- state: float32 [4, 256, 14, 16, 256], P('xs', 'bx'), may hold values from -6 to 6
- diffusivity: float32 [4, 256, 16, 256], P('xs', 'bx'), may hold values from 0.5 to 2
- velocity: float32 [4, 256, 3, 16, 256], P('xs', 'bx'), may hold values from -1 to 1
- species_scale: float32 [14], replicated, may hold values from 0.5 to 2
- new_owner: int32 [256], replicated, may hold values from 0 to 31, as said below
Outputs:
- advanced: float32 [4, 1280, 14, 16, 256], P('xs', 'bx')
The draws below stay inside these ranges and needn't reach their ends.
Inputs may be any that keep to these rules, and one draw needn't show every extreme that they name: `new_owner`: box b starts at owner b // 8. No two boxes of one starting owner go to the same other owner, and in every draw some owner receives a box from every other starting owner.
All inputs are finite; a program needn't handle non-finite values.
Results may differ from the reference program's by a relative error of at most 0.00002.
Values sent between devices are 32-bit elements; how exact they have to be, the bound alone decides.
A program may use at most 384 MiB of HBM per device.

```python
import math
import jax
import jax.numpy as jnp
from jax import lax

F = 14
BS = 16
BOX_DEV = 8
BOXES = 256
SLOTS = 40
N_XS = 4
N_BX = 32


def draw_new_owner(key, part):
    owners = BOXES // BOX_DEV
    key_hot, key_perm, key_move, key_force = jax.random.split(jax.random.fold_in(key, 11), 4)
    hot = jax.random.randint(key_hot, (), 0, owners)
    home = jnp.arange(owners, dtype=jnp.int32)
    orders = jax.vmap(lambda k: jax.random.permutation(k, owners - 1))(jax.random.split(key_perm, owners)) + 1
    hot_offset = (hot - home) % owners
    leading = orders[:, :1]
    orders = jnp.where(orders == hot_offset[:, None], leading, orders)
    orders = orders.at[:, 0].set(jnp.where(hot_offset > 0, hot_offset, orders[:, 0]))
    moving = jax.random.randint(key_move, (owners, BOX_DEV), 0, 4) < 3
    forced = jax.random.randint(key_force, (owners,), 0, BOX_DEV)
    moving = moving | (jnp.arange(BOX_DEV)[None, :] == forced[:, None])
    ranks = jnp.cumsum(moving.astype(jnp.int32), axis=1) - 1
    moving = moving & (ranks < owners - 1)
    offsets = jnp.take_along_axis(orders, jnp.clip(ranks, 0, owners - 2), axis=1)
    target = jnp.where(moving, (home[:, None] + offsets) % owners, home[:, None])
    return target.reshape(-1).astype(jnp.int32)


def levels(stream_key, shape, shards, smallest, high):
    factor_of, own = 1.0, jax.random.fold_in(stream_key, 6)
    for axis_at, blocks in shards:
        draws = jnp.exp(jax.random.uniform(jax.random.fold_in(own, axis_at), (blocks,), jnp.float32, smallest / len(shards), high / len(shards)))
        factor_of = factor_of * jnp.repeat(draws, shape[axis_at] // blocks).reshape([-1 if axis == axis_at else 1 for axis in range(len(shape))])
    return factor_of


def centred(stream_key, extent, scale, bound, pieces=(), held_as=jnp.bfloat16):
    values = scale * jax.random.normal(stream_key, extent, jnp.float32)
    if pieces:
        values = values * levels(stream_key, extent, pieces, -0.22, 0.18)
    return jnp.clip(values, -bound, bound).astype(held_as)


def setup_inputs(seed: int = 0) -> dict:
    key_list = jax.random.split(jax.random.key(seed), 6)
    state = centred(key_list[0], (N_XS, BOXES, F, BS, BS * BS), 1.0, 6.0, ((0, 4), (1, 32)), jnp.float32)
    diffusivity = jnp.clip(jnp.exp(math.log(2.0) - 1.3862944 * jax.random.uniform(key_list[1], (N_XS, BOXES, BS, BS * BS), jnp.float32) ** levels(key_list[1], (N_XS, BOXES, BS, BS * BS), ((0, 4), (1, 32)), -0.2, 0.2)), 0.5, 2.0)
    velocity = jnp.clip(jax.random.uniform(key_list[2], (N_XS, BOXES, 3, BS, BS * BS), jnp.float32, -1.0, 1.0) * levels(key_list[2], (N_XS, BOXES, 3, BS, BS * BS), ((0, 4), (1, 32)), -0.4, 0.0), -1.0, 1.0)
    species_scale = jnp.clip(jnp.exp(jax.random.uniform(key_list[3], (F,), jnp.float32, math.log(0.5), math.log(2.0))), 0.5, 2.0)
    new_owner = draw_new_owner(jax.random.fold_in(key_list[5], 71), 0)
    return dict(state=state, diffusivity=diffusivity, velocity=velocity, species_scale=species_scale, new_owner=new_owner)


time_step = 0.03

def neighbours(field, side):
    lanes = field.shape[-1]
    coord = lax.broadcasted_iota(jnp.int32, (lanes,), 0) % side
    up_y = jnp.concatenate([field[..., side:], field[..., lanes - side:]], axis=-1)
    down_y = jnp.concatenate([field[..., :side], field[..., :lanes - side]], axis=-1)
    up_z = jnp.concatenate([field[..., 1:], field[..., lanes - 1:]], axis=-1)
    down_z = jnp.concatenate([field[..., :1], field[..., :lanes - 1]], axis=-1)
    up_z = jnp.where(coord == side - 1, field, up_z)
    down_z = jnp.where(coord == 0, field, down_z)
    return (up_y, down_y, up_z, down_z)

def advance(conserved, diffusivity, velocity, scale):
    side = math.isqrt(conserved.shape[-1])
    center = conserved[..., 1:-1, :]
    ahead = conserved[..., 2:, :]
    behind = conserved[..., :-2, :]
    kappa = diffusivity[..., 1:-1, :]
    kappa_ahead = diffusivity[..., 2:, :]
    kappa_behind = diffusivity[..., :-2, :]
    q_up_y, q_down_y, q_up_z, q_down_z = neighbours(center, side)
    k_up_y, k_down_y, k_up_z, k_down_z = neighbours(kappa, side)
    spread = (kappa + kappa_ahead) * (ahead - center) + (kappa + kappa_behind) * (behind - center)
    spread = spread + (kappa + k_up_y) * (q_up_y - center) + (kappa + k_down_y) * (q_down_y - center)
    spread = spread + (kappa + k_up_z) * (q_up_z - center) + (kappa + k_down_z) * (q_down_z - center)
    spread = 0.5 * spread
    flow = velocity[..., 1:-1, :]
    along_x = flow[..., 0:1, :, :]
    along_y = flow[..., 1:2, :, :]
    along_z = flow[..., 2:3, :, :]
    transport = jnp.maximum(along_x, 0.0) * (center - behind) + jnp.minimum(along_x, 0.0) * (ahead - center)
    transport = transport + jnp.maximum(along_y, 0.0) * (center - q_down_y) + jnp.minimum(along_y, 0.0) * (q_up_y - center)
    transport = transport + jnp.maximum(along_z, 0.0) * (center - q_down_z) + jnp.minimum(along_z, 0.0) * (q_up_z - center)
    return center + time_step * (scale * spread - transport)

def periodic(values):
    return jnp.concatenate([values[:, -1:], values, values[:, :1]], axis=1)

def reference(state, diffusivity, velocity, species_scale, new_owner):
    scale = species_scale[:, None, None]
    lanes = BS * BS

    def pencil(items):
        cells, kappa, flow = items
        fields = jnp.transpose(cells, (1, 0, 2, 3)).reshape(F, N_XS * BS, lanes)
        coeff = kappa.reshape(1, N_XS * BS, lanes)
        speed = jnp.transpose(flow, (1, 0, 2, 3)).reshape(3, N_XS * BS, lanes)
        coeff_wide = periodic(coeff)
        speed_wide = periodic(speed)
        first = advance(periodic(fields), coeff_wide, speed_wide, scale)
        second = advance(periodic(first), coeff_wide, speed_wide, scale)
        return jnp.transpose(second.reshape(F, N_XS, BS, lanes), (1, 0, 2, 3))
    results = lax.map(pencil, (jnp.moveaxis(state, 1, 0), jnp.moveaxis(diffusivity, 1, 0), jnp.moveaxis(velocity, 1, 0)))
    boxes = jnp.arange(BOXES, dtype=jnp.int32)
    home = boxes // BOX_DEV
    within = boxes % BOX_DEV
    target = jnp.where(new_owner == home, new_owner * SLOTS + within, new_owner * SLOTS + BOX_DEV + home).astype(jnp.int32)
    output = jnp.zeros((N_XS, N_BX * SLOTS, F, BS, lanes), jnp.float32)
    return output.at[:, target].set(jnp.moveaxis(results, 0, 1))
```

```python
import functools

import jax
import jax.numpy as jnp
from jax import lax
from jax.experimental import pallas as pl
from jax.experimental.pallas import tpu as pltpu
from jax.sharding import PartitionSpec as P

MESH = pl.DeviceIdType.MESH
time_step = 0.03
SIDE = 16
LANES = SIDE * SIDE


def moved(q, shift):
    return pltpu.roll(q, (-shift) % LANES, q.ndim - 1)


def update(q, behind, ahead, load, s):
    spread = None
    for n, other in enumerate(
        (behind, ahead, moved(q, -SIDE), moved(q, SIDE), moved(q, -1), moved(q, 1))
    ):
        a, b = load(n)
        term = (s * a + b) * (other - q)
        spread = term if spread is None else spread + term
    return q + spread


def weights(k, k_behind, k_ahead, u, v, w, store):
    lane = lax.broadcasted_iota(jnp.int32, k.shape, k.ndim - 1)
    y, z = lane // SIDE, lane % SIDE
    sides = (
        (k_behind, u, False, None),
        (k_ahead, u, True, None),
        (moved(k, -SIDE), v, False, y > 0),
        (moved(k, SIDE), v, True, y < SIDE - 1),
        (moved(k, -1), w, False, z > 0),
        (moved(k, 1), w, True, z < SIDE - 1),
    )
    for n, (other, speed, up, inside) in enumerate(sides):
        a = (0.5 * time_step) * (k + other)
        b = (-time_step) * jnp.minimum(speed, 0.0) if up else time_step * jnp.maximum(speed, 0.0)
        if inside is not None:
            a, b = jnp.where(inside, a, 0.0), jnp.where(inside, b, 0.0)
        store(n, a, b)


def joined(q, first, last):
    rows = q.shape[0]
    row = lax.broadcasted_iota(jnp.int32, q.shape, 0)
    behind = jnp.where(row == 0, jnp.broadcast_to(first, q.shape), pltpu.roll(q, 1, 0))
    ahead = jnp.where(row == rows - 1, jnp.broadcast_to(last, q.shape), pltpu.roll(q, rows - 1, 0))
    return behind, ahead


def step_kernel(fields, boxes, scale, state, kappa, flow, res, up, down, low, high, wm, we, edge, send, recv):
    xs, bx, count = lax.axis_index("xs"), lax.axis_index("bx"), lax.axis_size("xs")
    after, before = (lax.rem(xs + 1, count), bx), (lax.rem(xs + count - 1, count), bx)
    barrier = pltpu.get_barrier_semaphore()
    for peer in (after, before):
        pl.semaphore_signal(barrier, inc=1, device_id=peer, device_id_type=MESH)

    far_k, near_k, near_v = 2 * fields, 2 * fields + 1, 2 * fields + 2
    for b in range(boxes):
        one = pl.ds(b, 1)
        for buf, far, near in ((up, SIDE - 2, SIDE - 1), (down, 1, 0)):

            @pl.loop(0, fields)
            def _(f, buf=buf, far=far, near=near, b=b, one=one):
                buf[f, one, :] = state[b, f, pl.ds(far, 1), :]
                buf[fields + f, one, :] = state[b, f, pl.ds(near, 1), :]

            buf[far_k, one, :] = kappa[b, pl.ds(far, 1), :]
            buf[near_k, one, :] = kappa[b, pl.ds(near, 1), :]
            for d in range(3):
                buf[near_v + d, one, :] = flow[b, d, pl.ds(near, 1), :]

    pl.semaphore_wait(barrier, 2)
    copies = [
        pltpu.make_async_remote_copy(
            src_ref=src, dst_ref=dst, send_sem=send.at[i], recv_sem=recv.at[i], device_id=peer, device_id_type=MESH
        )
        for i, (src, dst, peer) in enumerate(((up, low, after), (down, high, before)))
    ]
    for copy in copies:
        copy.start()
    for copy in copies:
        copy.wait()

    def keep(ref, at):
        def store(n, a, b):
            ref[(0, n) + at] = a
            ref[(1, n) + at] = b

        return store

    for i, (far, near, own) in enumerate(((low, low, down), (high, high, up))):
        ends = (far[far_k], own[near_k])
        weights(near[near_k], *(ends if i == 0 else ends[::-1]), *(near[near_v + d] for d in range(3)), keep(we, (i,)))
    for b in range(boxes):
        k = kappa[b]
        behind, ahead = joined(k, low[near_k, pl.ds(b, 1), :], high[near_k, pl.ds(b, 1), :])
        weights(k, behind, ahead, flow[b, 0], flow[b, 1], flow[b, 2], keep(wm, (b,)))

    @pl.loop(0, fields)
    def _(f):
        s = scale[f]
        for i, (halo, own) in enumerate(((low, down), (high, up))):
            ends = (halo[f], own[fields + f])
            edge[i] = update(
                halo[fields + f], *(ends if i == 0 else ends[::-1]), lambda n: (we[0, n, i], we[1, n, i]), s
            )
        for b in range(boxes):
            load = lambda n: (wm[0, n, b], wm[1, n, b])
            one = pl.ds(b, 1)
            q = state[b, f]
            q = update(q, *joined(q, low[fields + f, one, :], high[fields + f, one, :]), load, s)
            res[f, b] = update(q, *joined(q, edge[0, one, :], edge[1, one, :]), load, s)


def two_steps(state, kappa, flow, scale):
    boxes, fields = state.shape[:2]
    halo = pltpu.VMEM((2 * fields + 5, boxes, LANES), jnp.float32)
    vmem = pl.BlockSpec(memory_space=pltpu.VMEM)
    return pl.pallas_call(
        functools.partial(step_kernel, fields, boxes),
        out_shape=jax.ShapeDtypeStruct((fields, boxes, SIDE, LANES), jnp.float32),
        in_specs=[pl.BlockSpec(memory_space=pltpu.SMEM), vmem, vmem, vmem],
        out_specs=vmem,
        scratch_shapes=[
            halo,
            halo,
            halo,
            halo,
            pltpu.VMEM((2, 6, boxes, SIDE, LANES), jnp.float32),
            pltpu.VMEM((2, 6, 2, boxes, LANES), jnp.float32),
            pltpu.VMEM((2, boxes, LANES), jnp.float32),
            pltpu.SemaphoreType.DMA((2,)),
            pltpu.SemaphoreType.DMA((2,)),
        ],
        compiler_params=pltpu.CompilerParams(collective_id=0, has_side_effects=True, vmem_limit_bytes=40 << 20),
        name="two_steps",
    )(scale, state, kappa, flow)


def on_device(state, diffusivity, velocity, species_scale, new_owner):
    owners = lax.axis_size("bx")
    here = lax.axis_index("bx")
    holding = state.shape[1]
    local_owner = lax.dynamic_slice_in_dim(new_owner, here * holding, holding)
    moving = local_owner != here
    targets = jnp.arange(owners, dtype=jnp.int32)
    picked = (local_owner[None, :] == targets[:, None]) & moving[None, :]
    source_slot = jnp.sum(jnp.where(picked, jnp.arange(holding, dtype=jnp.int32)[None, :], 0), axis=1)
    present = jnp.any(picked, axis=1)
    staying = jnp.logical_not(moving).reshape(holding, 1, 1, 1)
    result = jnp.swapaxes(two_steps(state[0], diffusivity[0], velocity[0], species_scale), 0, 1)
    chosen = jnp.stack([lax.dynamic_index_in_dim(result, source_slot[o], 0, keepdims=False) for o in range(owners)])
    arrived = lax.all_to_all(
        jnp.where(present.reshape(owners, 1, 1, 1), chosen, 0.0), "bx", split_axis=0, concat_axis=0, tiled=True
    )
    return jnp.concatenate([jnp.where(staying, result, 0.0), arrived], axis=0)[None]


def solution(mesh):
    in_specs = (
        P("xs", "bx", None, None, None),
        P("xs", "bx", None, None),
        P("xs", "bx", None, None, None),
        P(),
        P(),
    )
    out_specs = P("xs", "bx", None, None, None)
    return jax.shard_map(on_device, mesh=mesh, in_specs=in_specs, out_specs=out_specs, check_vma=False)
```

```python
import functools

import jax
import jax.numpy as jnp
from jax import lax
from jax.experimental import pallas as pl
from jax.experimental.pallas import tpu as pltpu
from jax.sharding import PartitionSpec as P

MESH = pl.DeviceIdType.MESH
time_step = 0.03
SIDE = 16
LANES = SIDE * SIDE


def moved(q, shift):
    return pltpu.roll(q, (-shift) % LANES, q.ndim - 1)


def update(q, behind, ahead, load, s):
    spread = None
    for n, other in enumerate(
        (behind, ahead, moved(q, -SIDE), moved(q, SIDE), moved(q, -1), moved(q, 1))
    ):
        a, b = load(n)
        term = (s * a + b) * (other - q)
        spread = term if spread is None else spread + term
    return q + spread


def weights(k, k_behind, k_ahead, u, v, w, store):
    lane = lax.broadcasted_iota(jnp.int32, k.shape, k.ndim - 1)
    y, z = lane // SIDE, lane % SIDE
    sides = (
        (k_behind, u, False, None),
        (k_ahead, u, True, None),
        (moved(k, -SIDE), v, False, y > 0),
        (moved(k, SIDE), v, True, y < SIDE - 1),
        (moved(k, -1), w, False, z > 0),
        (moved(k, 1), w, True, z < SIDE - 1),
    )
    for n, (other, speed, up, inside) in enumerate(sides):
        a = (0.5 * time_step) * (k + other)
        b = (-time_step) * jnp.minimum(speed, 0.0) if up else time_step * jnp.maximum(speed, 0.0)
        if inside is not None:
            a, b = jnp.where(inside, a, 0.0), jnp.where(inside, b, 0.0)
        store(n, a, b)


def joined(q, first, last):
    rows = q.shape[0]
    row = lax.broadcasted_iota(jnp.int32, q.shape, 0)
    behind = jnp.where(row == 0, jnp.broadcast_to(first, q.shape), pltpu.roll(q, 1, 0))
    ahead = jnp.where(row == rows - 1, jnp.broadcast_to(last, q.shape), pltpu.roll(q, rows - 1, 0))
    return behind, ahead


I32 = jnp.int32
CAPS = (7, 6, 11, 8)
RING = 4
TABLE = 256
FINAL = 128


def count(mask):
    return jnp.sum(jnp.where(mask, 1, 0), axis=0, keepdims=True)


def column(row):
    n = row.shape[1]
    eye = lax.broadcasted_iota(I32, (n, n), 0) == lax.broadcasted_iota(I32, (n, n), 1)
    return jnp.sum(jnp.where(eye, row, 0), axis=1, keepdims=True)


def hops(at, d, node_up, node_down, first, second):
    n = at.shape[1]
    earlier = lax.broadcasted_iota(I32, (n, n), 0) < lax.broadcasted_iota(I32, (n, n), 1)
    at_c, d_c = column(at), column(d)
    here = at_c == at
    n1, n2, n3 = (count(here & (d_c == k)) for k in (1, 2, 3))
    r = count(here & (d_c == d) & earlier)
    half = jnp.clip((n2 + n3 - n1 + 1) >> 1, 0, n2)
    two = d == 2
    up = jnp.where(two, jnp.where(r < half, 1, 0), jnp.where(d == 1, 1, 0))
    rank = jnp.where(two, jnp.where(r < half, r, r - half), jnp.where(d == 1, half + r, n2 - half + r))
    mid = jnp.where(up == 1, node_up, node_down)
    local = count((at_c == mid) & (column(up) == up) & (d_c > 0))
    late = rank >= first
    slot = jnp.where(two, jnp.maximum(local - first, 0) + rank, rank - first)
    lost = (two & (late | (slot >= second))) | ((d > 0) & jnp.logical_not(two) & (slot >= second))
    return up, rank, late, slot, mid, jnp.sum(jnp.where(lost, 1, 0), keepdims=True)


def plan(owner, z, y, net):
    n = owner.shape[1]
    ka, kb, kc, kd = CAPS
    b = lax.broadcasted_iota(I32, owner.shape, 1)
    home = b // 8
    moving = owner != home

    def pq(chip):
        return (chip % RING, chip // RING) if net == 0 else (chip // RING, chip % RING)

    node = lambda p, q: p * RING + q
    p0, q0 = pq(home // 2)
    p1, q1 = pq(jnp.where(moving, owner, home) // 2)
    me = node(y, z) if net == 0 else node(z, y)
    turn = lambda p, k: (p + k) % RING
    base_a = 16
    base_b = base_a + 2 * ka
    base_c = base_b + 2 * kb
    base_d = base_c + 2 * kc
    own = b % 16
    d1 = turn(p1 - p0, RING)
    up1, rank1, late1, slot1, mid1, lost1 = hops(
        node(p0, q0), d1, node(turn(p0, 1), q0), node(turn(p0, 3), q0), ka, kb
    )
    in_a = base_a + (1 - up1) * ka + rank1
    at1 = jnp.where(d1 == 0, own, jnp.where((d1 == 2) | late1, base_b + (1 - up1) * kb + slot1, in_a))
    d2 = turn(q1 - q0, RING)
    up2, rank2, late2, slot2, mid2, lost2 = hops(
        node(p1, q0), d2, node(p1, turn(q0, 1)), node(p1, turn(q0, 3)), kc, kd
    )
    in_c = base_c + (1 - up2) * kc + rank2
    at2 = jnp.where(d2 == 0, at1, jnp.where((d2 == 2) | late2, base_d + (1 - up2) * kd + slot2, in_c))
    nodes = (node(p0, q0), node(p1, q0), node(p1, q1))
    entries = (
        ((nodes[0] == me) & (d1 > 0) & jnp.logical_not(late1), (1 - up1) * ka + rank1, own),
        ((nodes[0] == me) & (d1 > 0) & (d1 != 2) & late1, 2 * ka + (1 - up1) * kb + slot1, own),
        ((mid1 == me) & (d1 == 2), 2 * ka + (1 - up1) * kb + slot1, in_a),
        ((nodes[1] == me) & (d2 > 0) & jnp.logical_not(late2), 2 * (ka + kb) + (1 - up2) * kc + rank2, at1),
        ((nodes[1] == me) & (d2 > 0) & (d2 != 2) & late2, 2 * (ka + kb + kc) + (1 - up2) * kd + slot2, at1),
        ((mid2 == me) & (d2 == 2), 2 * (ka + kb + kc) + (1 - up2) * kd + slot2, in_c),
        ((nodes[2] == me) & moving, FINAL + (owner % 2) * 32 + home, at2 + 1),
    )
    lane = lax.broadcasted_iota(I32, (n, TABLE), 1)
    table = jnp.where(lax.broadcasted_iota(I32, (1, TABLE), 1) >= FINAL, -1, 0)
    for mask, slot, place in entries:
        slot, place = column(jnp.where(mask, slot, -1)), column(place)
        table = table + jnp.sum(jnp.where(lane == slot, place, 0), axis=0, keepdims=True)
    top = 16 + 2 * sum(CAPS) - 1
    return jnp.clip(table, -1, top), lost1 + lost2


def plan_kernel(owner, table):
    bx = lax.axis_index("bx")
    chip, core = bx // 2, bx % 2
    z, y = chip // RING, chip % RING
    one, lost_one = plan(owner[...], z, y, 0)
    two, lost_two = plan(owner[...], z, y, 1)
    lost = lost_one + lost_two
    row = jnp.where(core == 0, one, two)
    lane = lax.broadcasted_iota(I32, row.shape, 1)
    table[...] = jnp.where(lane == TABLE - 1, jnp.broadcast_to(lost, row.shape), row)


def make_plan(new_owner):
    vmem = pl.BlockSpec(memory_space=pltpu.VMEM)
    return pl.pallas_call(
        plan_kernel,
        out_shape=jax.ShapeDtypeStruct((1, TABLE), I32),
        in_specs=[vmem],
        out_specs=vmem,
        name="plan",
    )(new_owner.reshape(1, -1))


def regrid_kernel(
    fields, boxes, homes, table, owner, scale, state_hbm, kappa_hbm, flow_hbm, res, stay, near_out, far_out,
    state, kappa, flow, up, down, low, high, wm, we, edge, sib, pool, fin, sa, sb, sc, sd, ra, rb, rc, rd,
    in_sem, halo_sem, sib_sem, fin_sem, send, recv,
):
    xs, bx, n_xs = lax.axis_index("xs"), lax.axis_index("bx"), lax.axis_size("xs")
    chip, core = bx // 2, bx % 2
    z, y = chip // RING, chip % RING
    half = fields // 2

    def device(dz, dy):
        return (xs, (((z + dz) % RING) * RING + (y + dy) % RING) * 2 + core)

    def peer(ring, step):
        along_y = (1 - core) if ring == 0 else core
        return device(step * (1 - along_y), step * along_y)

    sibling = (xs, bx + 1 - 2 * core)
    after, before = (lax.rem(xs + 1, n_xs), bx), (lax.rem(xs + n_xs - 1, n_xs), bx)
    around = [peer(ring, step) for ring in (0, 1) for step in (1, RING - 1)]
    barrier = pltpu.get_barrier_semaphore()
    for other in (after, before, sibling, *around):
        pl.semaphore_signal(barrier, inc=1, device_id=other, device_id_type=MESH)
    loads = [
        pltpu.make_async_copy(src, dst, in_sem.at[i])
        for i, (src, dst) in enumerate(((state_hbm, state), (kappa_hbm, kappa), (flow_hbm, flow)))
    ]
    for copy in loads:
        copy.start()
    for copy in loads:
        copy.wait()

    far_k, near_k, near_v = 2 * fields, 2 * fields + 1, 2 * fields + 2
    for b in range(boxes):
        one = pl.ds(b, 1)
        for buf, far, near in ((up, SIDE - 2, SIDE - 1), (down, 1, 0)):

            @pl.loop(0, fields)
            def _(f, buf=buf, far=far, near=near, b=b, one=one):
                buf[f, one, :] = state[b, f, pl.ds(far, 1), :]
                buf[fields + f, one, :] = state[b, f, pl.ds(near, 1), :]

            buf[far_k, one, :] = kappa[b, pl.ds(far, 1), :]
            buf[near_k, one, :] = kappa[b, pl.ds(near, 1), :]
            for d in range(3):
                buf[near_v + d, one, :] = flow[b, d, pl.ds(near, 1), :]

    pl.semaphore_wait(barrier, 3 + len(around))
    copies = [
        pltpu.make_async_remote_copy(
            src_ref=src,
            dst_ref=dst,
            send_sem=halo_sem.at[0, i],
            recv_sem=halo_sem.at[1, i],
            device_id=other,
            device_id_type=MESH,
        )
        for i, (src, dst, other) in enumerate(((up, low, after), (down, high, before)))
    ]
    for copy in copies:
        copy.start()
    for copy in copies:
        copy.wait()

    def keep(ref, at):
        def store(n, a, b):
            ref[(0, n) + at] = a
            ref[(1, n) + at] = b

        return store

    for i, (far, near, own) in enumerate(((low, low, down), (high, high, up))):
        ends = (far[far_k], own[near_k])
        weights(near[near_k], *(ends if i == 0 else ends[::-1]), *(near[near_v + d] for d in range(3)), keep(we, (i,)))
    for b in range(boxes):
        k = kappa[b]
        behind, ahead = joined(k, low[near_k, pl.ds(b, 1), :], high[near_k, pl.ds(b, 1), :])
        weights(k, behind, ahead, flow[b, 0], flow[b, 1], flow[b, 2], keep(wm, (b,)))

    def advance(f):
        s = scale[f]
        for i, (halo, own) in enumerate(((low, down), (high, up))):
            ends = (halo[f], own[fields + f])
            edge[i] = update(
                halo[fields + f], *(ends if i == 0 else ends[::-1]), lambda n: (we[0, n, i], we[1, n, i]), s
            )
        for b in range(boxes):
            load = lambda n: (wm[0, n, b], wm[1, n, b])
            one = pl.ds(b, 1)
            q = state[b, f]
            q = update(q, *joined(q, low[fields + f, one, :], high[fields + f, one, :]), load, s)
            q = update(q, *joined(q, edge[0, one, :], edge[1, one, :]), load, s)
            res[f, b] = q
            stay[f, b] = jnp.where(owner[bx * boxes + b] == bx, q, 0.0)

    def to_sibling(t):
        return pltpu.make_async_remote_copy(
            src_ref=res.at[(1 - core) * half + t],
            dst_ref=sib.at[t],
            send_sem=sib_sem.at[0, t],
            recv_sem=sib_sem.at[1, t],
            device_id=sibling,
            device_id_type=MESH,
        )

    def back(t):
        return pltpu.make_async_remote_copy(
            src_ref=fin.at[t],
            dst_ref=far_out.at[t],
            send_sem=fin_sem.at[0, t],
            recv_sem=fin_sem.at[1, t],
            device_id=sibling,
            device_id_type=MESH,
        )

    outgoing, incoming = (sa, sb, sc, sd), (ra, rb, rc, rd)
    start = [2 * sum(CAPS[:i]) for i in range(4)]

    def hop(stage, way, t):
        return pltpu.make_async_remote_copy(
            src_ref=outgoing[stage].at[t, way],
            dst_ref=incoming[stage].at[t, way],
            send_sem=send.at[stage, way, t],
            recv_sem=recv.at[stage, way, t],
            device_id=around[(stage // 2) * 2 + way],
            device_id_type=MESH,
        )

    def compute(t):
        @pl.loop(0, 2)
        def _(i):
            advance(i * half + t)

        to_sibling(t).start()

    def gather(stage, t):
        for way in (0, 1):
            for k in range(CAPS[stage]):
                outgoing[stage][t, way, k] = pool[t, table[0, start[stage] + way * CAPS[stage] + k]]
            hop(stage, way, t).start()

    def take(stage, t):
        for way in (0, 1):
            hop(stage, way, t).wait_recv()
            pool[t, pl.ds(16 + start[stage] + way * CAPS[stage], CAPS[stage])] = incoming[stage][t, way]

    def first(t):
        to_sibling(t).wait_recv()
        pool[t, pl.ds(core * boxes, boxes)] = res[core * half + t]
        pool[t, pl.ds((1 - core) * boxes, boxes)] = sib[t]
        gather(0, t)

    def middle(stage):
        def run(t):
            take(stage - 1, t)
            gather(stage, t)

        return run

    def last(t):
        take(3, t)
        for dst, whose in ((fin, 1 - core), (near_out, core)):

            @pl.loop(0, homes)
            def _(h, dst=dst, whose=whose):
                place = table[0, FINAL + whose * 32 + h]
                dst[t, h] = jnp.where(place >= 0, pool[t, jnp.maximum(place, 0)], 0.0)

            if dst is fin:
                back(t).start()

    steps = (first, middle(1), middle(2), middle(3), last)
    compute(0)

    @pl.loop(0, half + len(steps) - 1)
    def _(t):
        for lag, run in enumerate(steps):

            @pl.when((t >= lag) & (t < half + lag))
            def _(run=run, lag=lag):
                run(t - lag)

        @pl.when(t + 1 < half)
        def _():
            compute(t + 1)

    @pl.loop(0, half)
    def _(t):
        to_sibling(t).wait_send()
        back(t).wait()
        for stage in range(4):
            for way in (0, 1):
                hop(stage, way, t).wait_send()


def regrid(table, new_owner, scale, state, kappa, flow):
    boxes, fields = state.shape[:2]
    homes = new_owner.shape[0] // boxes
    half = fields // 2
    f32 = jnp.float32
    vmem, smem, hbm = (pl.BlockSpec(memory_space=m) for m in (pltpu.VMEM, pltpu.SMEM, pltpu.HBM))
    box = (SIDE, LANES)
    halo = pltpu.VMEM((2 * fields + 5, boxes, LANES), f32)
    slots = [pltpu.VMEM((half, 2, k) + box, f32) for k in CAPS]
    dma = pltpu.SemaphoreType.DMA
    return pl.pallas_call(
        functools.partial(regrid_kernel, fields, boxes, homes),
        out_shape=[jax.ShapeDtypeStruct((fields, boxes) + box, f32)] * 2
        + [jax.ShapeDtypeStruct((half, homes) + box, f32)] * 2,
        in_specs=[smem, smem, smem, hbm, hbm, hbm],
        out_specs=[vmem] * 4,
        scratch_shapes=[
            pltpu.VMEM((boxes, fields) + box, f32),
            pltpu.VMEM((boxes,) + box, f32),
            pltpu.VMEM((boxes, 3) + box, f32),
            halo,
            halo,
            halo,
            halo,
            pltpu.VMEM((2, 6, boxes) + box, f32),
            pltpu.VMEM((2, 6, 2, boxes, LANES), f32),
            pltpu.VMEM((2, boxes, LANES), f32),
            pltpu.VMEM((half, boxes) + box, f32),
            pltpu.VMEM((half, 16 + 2 * sum(CAPS)) + box, f32),
            pltpu.VMEM((half, homes) + box, f32),
            *slots,
            *slots,
            dma((3,)),
            dma((2, 2)),
            dma((2, half)),
            dma((2, half)),
            dma((4, 2, half)),
            dma((4, 2, half)),
        ],
        compiler_params=pltpu.CompilerParams(collective_id=0, has_side_effects=True, vmem_limit_bytes=48 << 20),
        name="regrid",
    )(table, new_owner, scale, state, kappa, flow)


def place_kernel(stay, near, far, out):
    core = lax.axis_index("bx") % 2
    boxes = stay.shape[2]
    for b in range(boxes):
        for group in (0, 1):
            out[b, group, 0] = stay[group, 0, b]
    out[boxes:, core, 0] = near[0]
    out[boxes:, 1 - core, 0] = far[0]


def placed(stay, near, far):
    fields, boxes = stay.shape[:2]
    half, homes = near.shape[:2]
    box = stay.shape[2:]
    arrived = pl.BlockSpec((1, homes) + box, lambda t: (t, 0, 0, 0))
    out = pl.pallas_call(
        place_kernel,
        grid=(half,),
        out_shape=jax.ShapeDtypeStruct((boxes + homes, 2, half) + box, stay.dtype),
        in_specs=[pl.BlockSpec((2, 1, boxes) + box, lambda t: (0, t, 0, 0, 0)), arrived, arrived],
        out_specs=pl.BlockSpec((boxes + homes, 2, 1) + box, lambda t: (0, 0, t, 0, 0)),
        compiler_params=pltpu.CompilerParams(vmem_limit_bytes=16 << 20),
        name="placed",
    )(stay.reshape((2, half, boxes) + box), near, far)
    return out.reshape((boxes + homes, fields) + box)


def dense(result, new_owner):
    owners, here = lax.axis_size("bx"), lax.axis_index("bx")
    holding = result.shape[1]
    local_owner = lax.dynamic_slice_in_dim(new_owner, here * holding, holding)
    moving = local_owner != here
    targets = jnp.arange(owners, dtype=I32)
    picked = (local_owner[None, :] == targets[:, None]) & moving[None, :]
    source = jnp.sum(jnp.where(picked, jnp.arange(holding, dtype=I32)[None, :], 0), axis=1)
    present = jnp.any(picked, axis=1).reshape(owners, 1, 1, 1)
    result = jnp.swapaxes(result, 0, 1)
    chosen = lax.map(lambda i: lax.dynamic_index_in_dim(result, i, 0, keepdims=False), source)
    arrived = lax.all_to_all(jnp.where(present, chosen, 0.0), "bx", split_axis=0, concat_axis=0, tiled=True)
    staying = jnp.logical_not(moving).reshape(holding, 1, 1, 1)
    return jnp.concatenate([jnp.where(staying, result, 0.0), arrived], axis=0)


def on_device(state, diffusivity, velocity, species_scale, new_owner):
    table = make_plan(new_owner)
    res, stay, near, far = regrid(table, new_owner, species_scale, state[0], diffusivity[0], velocity[0])
    result = lax.cond(
        table[0, TABLE - 1] == 0,
        lambda res, stay, near, far: placed(stay, near, far),
        lambda res, stay, near, far: dense(res, new_owner),
        res,
        stay,
        near,
        far,
    )
    return result[None]


def solution(mesh):
    in_specs = (
        P("xs", "bx", None, None, None),
        P("xs", "bx", None, None),
        P("xs", "bx", None, None, None),
        P(),
        P(),
    )
    out_specs = P("xs", "bx", None, None, None)
    return jax.shard_map(on_device, mesh=mesh, in_specs=in_specs, out_specs=out_specs, check_vma=False)
```

```python
import functools

import jax
import jax.numpy as jnp
from jax import lax
from jax.experimental import pallas as pl
from jax.experimental.pallas import tpu as pltpu
from jax.sharding import PartitionSpec as P

MESH = pl.DeviceIdType.MESH
time_step = 0.03
SIDE = 16
LANES = SIDE * SIDE


def moved(q, shift):
    return pltpu.roll(q, (-shift) % LANES, q.ndim - 1)


def update(q, behind, ahead, load, s):
    spread = None
    for n, other in enumerate(
        (behind, ahead, moved(q, -SIDE), moved(q, SIDE), moved(q, -1), moved(q, 1))
    ):
        a, b = load(n)
        term = (s * a + b) * (other - q)
        spread = term if spread is None else spread + term
    return q + spread


def weights(k, k_behind, k_ahead, u, v, w, store):
    lane = lax.broadcasted_iota(jnp.int32, k.shape, k.ndim - 1)
    y, z = lane // SIDE, lane % SIDE
    sides = (
        (k_behind, u, False, None),
        (k_ahead, u, True, None),
        (moved(k, -SIDE), v, False, y > 0),
        (moved(k, SIDE), v, True, y < SIDE - 1),
        (moved(k, -1), w, False, z > 0),
        (moved(k, 1), w, True, z < SIDE - 1),
    )
    for n, (other, speed, up, inside) in enumerate(sides):
        a = (0.5 * time_step) * (k + other)
        b = (-time_step) * jnp.minimum(speed, 0.0) if up else time_step * jnp.maximum(speed, 0.0)
        if inside is not None:
            a, b = jnp.where(inside, a, 0.0), jnp.where(inside, b, 0.0)
        store(n, a, b)


def joined(q, first, last):
    rows = q.shape[0]
    row = lax.broadcasted_iota(jnp.int32, q.shape, 0)
    behind = jnp.where(row == 0, jnp.broadcast_to(first, q.shape), pltpu.roll(q, 1, 0))
    ahead = jnp.where(row == rows - 1, jnp.broadcast_to(last, q.shape), pltpu.roll(q, rows - 1, 0))
    return behind, ahead


I32 = jnp.int32
CAPS = (7, 6, 11, 8)
RING = 4
TABLE = 256
FINAL = 128
NONE = 16 + 2 * sum(CAPS)


def count(mask):
    return jnp.sum(jnp.where(mask, 1, 0), axis=0, keepdims=True)


def column(row):
    n = row.shape[1]
    eye = lax.broadcasted_iota(I32, (n, n), 0) == lax.broadcasted_iota(I32, (n, n), 1)
    return jnp.sum(jnp.where(eye, row, 0), axis=1, keepdims=True)


def hops(at, d, node_up, node_down, first, second):
    n = at.shape[1]
    earlier = lax.broadcasted_iota(I32, (n, n), 0) < lax.broadcasted_iota(I32, (n, n), 1)
    at_c, d_c = column(at), column(d)
    here = at_c == at
    n1, n2, n3 = (count(here & (d_c == k)) for k in (1, 2, 3))
    r = count(here & (d_c == d) & earlier)
    half = jnp.clip((n2 + n3 - n1 + 1) >> 1, 0, n2)
    two = d == 2
    up = jnp.where(two, jnp.where(r < half, 1, 0), jnp.where(d == 1, 1, 0))
    rank = jnp.where(two, jnp.where(r < half, r, r - half), jnp.where(d == 1, half + r, n2 - half + r))
    mid = jnp.where(up == 1, node_up, node_down)
    local = count((at_c == mid) & (column(up) == up) & (d_c > 0))
    late = rank >= first
    slot = jnp.where(two, jnp.maximum(local - first, 0) + rank, rank - first)
    lost = (two & (late | (slot >= second))) | ((d > 0) & jnp.logical_not(two) & (slot >= second))
    return up, rank, late, slot, mid, jnp.sum(jnp.where(lost, 1, 0), keepdims=True)


def plan(owner, z, y, net):
    n = owner.shape[1]
    ka, kb, kc, kd = CAPS
    b = lax.broadcasted_iota(I32, owner.shape, 1)
    home = b // 8
    moving = owner != home

    def pq(chip):
        return (chip % RING, chip // RING) if net == 0 else (chip // RING, chip % RING)

    node = lambda p, q: p * RING + q
    p0, q0 = pq(home // 2)
    p1, q1 = pq(jnp.where(moving, owner, home) // 2)
    me = node(y, z) if net == 0 else node(z, y)
    turn = lambda p, k: (p + k) % RING
    base_a = 16
    base_b = base_a + 2 * ka
    base_c = base_b + 2 * kb
    base_d = base_c + 2 * kc
    own = b % 16
    d1 = turn(p1 - p0, RING)
    up1, rank1, late1, slot1, mid1, lost1 = hops(
        node(p0, q0), d1, node(turn(p0, 1), q0), node(turn(p0, 3), q0), ka, kb
    )
    in_a = base_a + (1 - up1) * ka + rank1
    at1 = jnp.where(d1 == 0, own, jnp.where((d1 == 2) | late1, base_b + (1 - up1) * kb + slot1, in_a))
    d2 = turn(q1 - q0, RING)
    up2, rank2, late2, slot2, mid2, lost2 = hops(
        node(p1, q0), d2, node(p1, turn(q0, 1)), node(p1, turn(q0, 3)), kc, kd
    )
    in_c = base_c + (1 - up2) * kc + rank2
    at2 = jnp.where(d2 == 0, at1, jnp.where((d2 == 2) | late2, base_d + (1 - up2) * kd + slot2, in_c))
    nodes = (node(p0, q0), node(p1, q0), node(p1, q1))
    entries = (
        ((nodes[0] == me) & (d1 > 0) & jnp.logical_not(late1), (1 - up1) * ka + rank1, own),
        ((nodes[0] == me) & (d1 > 0) & (d1 != 2) & late1, 2 * ka + (1 - up1) * kb + slot1, own),
        ((mid1 == me) & (d1 == 2), 2 * ka + (1 - up1) * kb + slot1, in_a),
        ((nodes[1] == me) & (d2 > 0) & jnp.logical_not(late2), 2 * (ka + kb) + (1 - up2) * kc + rank2, at1),
        ((nodes[1] == me) & (d2 > 0) & (d2 != 2) & late2, 2 * (ka + kb + kc) + (1 - up2) * kd + slot2, at1),
        ((mid2 == me) & (d2 == 2), 2 * (ka + kb + kc) + (1 - up2) * kd + slot2, in_c),
        ((nodes[2] == me) & moving, FINAL + (owner % 2) * 32 + home, at2 - NONE),
    )
    lane = lax.broadcasted_iota(I32, (n, TABLE), 1)
    table = jnp.where(lax.broadcasted_iota(I32, (1, TABLE), 1) >= FINAL, NONE, 0)
    for mask, slot, place in entries:
        slot, place = column(jnp.where(mask, slot, -1)), column(place)
        table = table + jnp.sum(jnp.where(lane == slot, place, 0), axis=0, keepdims=True)
    return jnp.clip(table, 0, NONE), lost1 + lost2


def both_plans(owner, z, y, core):
    one, lost_one = plan(owner, z, y, 0)
    two, lost_two = plan(owner, z, y, 1)
    row = jnp.where(core == 0, one, two)
    lane = lax.broadcasted_iota(I32, row.shape, 1)
    return jnp.where(lane == TABLE - 1, jnp.broadcast_to(jnp.minimum(lost_one + lost_two, 1), row.shape), row)


def regrid_kernel(
    fields, boxes, homes, owner_row, owner, scale, state_hbm, kappa_hbm, flow_hbm, out, res_hbm, lost,
    res, state, kappa, flow, up, down, low, high, wm, we, edge, sib, pool, fin, sa, sb, sc, sd, ra, rb, rc, rd,
    row, table, in_sem, halo_sem, halo_sent, sib_sem, sib_sent, fin_sem, keep_sem, send, recv,
):
    xs, bx, n_xs = lax.axis_index("xs"), lax.axis_index("bx"), lax.axis_size("xs")
    chip, core = bx // 2, bx % 2
    z, y = chip // RING, chip % RING
    half = fields // 2

    def device(dz, dy):
        return (xs, (((z + dz) % RING) * RING + (y + dy) % RING) * 2 + core)

    def peer(ring, step):
        along_y = (1 - core) if ring == 0 else core
        return device(step * (1 - along_y), step * along_y)

    sibling = (xs, bx + 1 - 2 * core)
    after, before = (lax.rem(xs + 1, n_xs), bx), (lax.rem(xs + n_xs - 1, n_xs), bx)
    around = [peer(ring, step) for ring in (0, 1) for step in (1, RING - 1)]
    barrier = pltpu.get_barrier_semaphore()
    for other in (after, before, sibling, *around):
        pl.semaphore_signal(barrier, inc=1, device_id=other, device_id_type=MESH)
    loads = [
        pltpu.make_async_copy(src, dst, in_sem.at[i])
        for i, (src, dst) in enumerate(((state_hbm, state), (kappa_hbm, kappa), (flow_hbm, flow)))
    ]
    for copy in loads:
        copy.start()
    for copy in loads:
        copy.wait()

    far_k, near_k, near_v = 2 * fields, 2 * fields + 1, 2 * fields + 2
    for buf, far, near in ((up, SIDE - 2, SIDE - 1), (down, 1, 0)):
        for b in range(boxes):
            one = pl.ds(b, 1)
            buf[far_k, one, :] = kappa[b, pl.ds(far, 1), :]
            buf[near_k, one, :] = kappa[b, pl.ds(near, 1), :]
            for d in range(3):
                buf[near_v + d, one, :] = flow[b, d, pl.ds(near, 1), :]

        @pl.loop(0, half)
        def _(t, buf=buf, far=far, near=near):
            for i in (0, 1):
                for side, row in enumerate((far, near)):
                    rows = [state[b, i * half + t, pl.ds(row, 1), :] for b in range(boxes)]
                    for b in range(boxes):
                        buf[4 * t + 2 * i + side, pl.ds(b, 1), :] = rows[b]

    pl.semaphore_wait(barrier, 3 + len(around))

    def ends_of(way, first, rows, part):
        src, dst, other = ((up, low, after), (down, high, before))[way]
        return pltpu.make_async_remote_copy(
            src_ref=src.at[pl.ds(first, rows)],
            dst_ref=dst.at[pl.ds(first, rows)],
            send_sem=halo_sent.at[way],
            recv_sem=halo_sem.at[way, part],
            device_id=other,
            device_id_type=MESH,
        )

    coefficients = [ends_of(way, far_k, 5, half) for way in (0, 1)]
    for copy in coefficients:
        copy.start()

    @pl.loop(0, half)
    def _(t):
        for way in (0, 1):
            ends_of(way, 4 * t, 4, t).start()

    row[...] = both_plans(owner_row[...], z, y, core)
    to_scalars = pltpu.make_async_copy(row, table, in_sem.at[3])
    to_scalars.start()
    for copy in coefficients:
        copy.wait_recv()

    def keep(ref, at):
        def store(n, a, b):
            ref[(0, n) + at] = a
            ref[(1, n) + at] = b

        return store

    for i, (far, near, own) in enumerate(((low, low, down), (high, high, up))):
        ends = (far[far_k], own[near_k])
        weights(near[near_k], *(ends if i == 0 else ends[::-1]), *(near[near_v + d] for d in range(3)), keep(we, (i,)))
    for b in range(boxes):
        k = kappa[b]
        behind, ahead = joined(k, low[near_k, pl.ds(b, 1), :], high[near_k, pl.ds(b, 1), :])
        weights(k, behind, ahead, flow[b, 0], flow[b, 1], flow[b, 2], keep(wm, (b,)))

    def advance(t, k):
        f = k * half + t
        s = scale[f]
        far, near = 4 * t + 2 * k, 4 * t + 2 * k + 1
        for i, (halo, own) in enumerate(((low, down), (high, up))):
            ends = (halo[far], own[near])
            edge[i] = update(halo[near], *(ends if i == 0 else ends[::-1]), lambda n: (we[0, n, i], we[1, n, i]), s)
        for b in range(boxes):
            load = lambda n: (wm[0, n, b], wm[1, n, b])
            one = pl.ds(b, 1)
            q = state[b, f]
            q = update(q, *joined(q, low[near, one, :], high[near, one, :]), load, s)
            q = update(q, *joined(q, edge[0, one, :], edge[1, one, :]), load, s)
            res[f, b] = q
            out[b, k, t] = jnp.where(owner[bx * boxes + b] == bx, q, 0.0)

    def to_sibling(src, dst, t):
        return pltpu.make_async_remote_copy(
            src_ref=src, dst_ref=dst, send_sem=sib_sent.at[0], recv_sem=sib_sem.at[t], device_id=sibling, device_id_type=MESH
        )

    def share(t):
        return to_sibling(res.at[(1 - core) * half + t], sib.at[t], t)

    def back(src, dst):
        return pltpu.make_async_remote_copy(
            src_ref=src, dst_ref=dst, send_sem=fin_sem.at[0], recv_sem=fin_sem.at[1], device_id=sibling, device_id_type=MESH
        )

    def kept(k, t):
        return pltpu.make_async_copy(res.at[k * half + t], res_hbm.at[:, k * half + t], keep_sem.at[k, t])

    outgoing, incoming = (sa, sb, sc, sd), (ra, rb, rc, rd)
    start = [2 * sum(CAPS[:i]) for i in range(4)]

    def hop(stage, way, t):
        return pltpu.make_async_remote_copy(
            src_ref=outgoing[stage].at[t, way],
            dst_ref=incoming[stage].at[t, way],
            send_sem=send.at[stage],
            recv_sem=recv.at[stage, way, t],
            device_id=around[(stage // 2) * 2 + way],
            device_id_type=MESH,
        )

    def compute(t):
        for way in (0, 1):
            ends_of(way, 4 * t, 4, t).wait_recv()

        @pl.loop(0, 2)
        def _(k):
            advance(t, k)

        share(t).start()
        kept(0, t).start()
        kept(1, t).start()

    def pick(t, first, places, store):
        for k in range(0, places, 6):
            group = range(k, min(k + 6, places))
            values = [pool[t, table[0, first + j]] for j in group]
            for j, value in zip(group, values):
                store(j, value)

    def gather(stage, t):
        slots = CAPS[stage]
        for way in (0, 1):

            def store(k, value, way=way):
                outgoing[stage][t, way, k] = value

            pick(t, start[stage] + way * slots, slots, store)
            hop(stage, way, t).start()

    def take(stage, t):
        for way in (0, 1):
            hop(stage, way, t).wait_recv()
            pool[t, pl.ds(16 + start[stage] + way * CAPS[stage], CAPS[stage])] = incoming[stage][t, way]

    def first(t):
        share(t).wait_recv()
        pool[t, pl.ds(core * boxes, boxes)] = res[core * half + t]
        pool[t, pl.ds((1 - core) * boxes, boxes)] = sib[t]
        pool[t, NONE] = jnp.zeros((SIDE, LANES), jnp.float32)
        gather(0, t)

    def middle(stage):
        def run(t):
            take(stage - 1, t)
            gather(stage, t)

        return run

    def last(t):
        take(3, t)

        def store_far(h, value):
            fin[t, h] = value

        def store_near(h, value):
            out[boxes + h, core, t] = value

        pick(t, FINAL + (1 - core) * 32, homes, store_far)
        back(fin.at[t], out.at[pl.ds(boxes, homes), core, t]).start()
        pick(t, FINAL + core * 32, homes, store_near)

    steps = (first, middle(1), middle(2), middle(3), last)
    compute(0)
    compute(1)
    to_scalars.wait()
    lost[0] = table[0, TABLE - 1]

    @pl.loop(0, half + len(steps) - 1)
    def _(t):
        for lag, run in enumerate(steps):

            @pl.when((t >= lag) & (t < half + lag))
            def _(run=run, lag=lag):
                run(t - lag)

        @pl.when(t + 2 < half)
        def _():
            compute(t + 2)

    for way, (src, other) in enumerate(((up, after), (down, before))):
        pltpu.make_async_remote_copy(
            src_ref=src,
            dst_ref=src,
            send_sem=halo_sent.at[way],
            recv_sem=halo_sem.at[way, 0],
            device_id=other,
            device_id_type=MESH,
        ).wait_send()
    to_sibling(sib, sib, 0).wait_send()
    back(fin, fin).wait()
    for stage in range(4):
        pltpu.make_async_remote_copy(
            src_ref=outgoing[stage],
            dst_ref=incoming[stage],
            send_sem=send.at[stage],
            recv_sem=recv.at[stage, 0, 0],
            device_id=sibling,
            device_id_type=MESH,
        ).wait_send()

    @pl.loop(0, half)
    def _(t):
        for k in (0, 1):
            kept(k, t).wait()


def regrid(new_owner, scale, state, kappa, flow):
    boxes, fields = state.shape[:2]
    homes = new_owner.shape[0] // boxes
    half = fields // 2
    f32 = jnp.float32
    vmem, smem, hbm = (pl.BlockSpec(memory_space=m) for m in (pltpu.VMEM, pltpu.SMEM, pltpu.HBM))
    box = (SIDE, LANES)
    halo = pltpu.VMEM((2 * fields + 5, boxes, LANES), f32)
    slots = [pltpu.VMEM((half, 2, k) + box, f32) for k in CAPS]
    dma = pltpu.SemaphoreType.DMA
    return pl.pallas_call(
        functools.partial(regrid_kernel, fields, boxes, homes),
        out_shape=[
            pltpu.VMEM((boxes + homes, 2, half) + box, f32),
            pltpu.HBM((boxes, fields) + box, f32),
            jax.ShapeDtypeStruct((1,), I32),
        ],
        in_specs=[vmem, smem, smem, hbm, hbm, hbm],
        out_specs=[vmem, hbm, smem],
        scratch_shapes=[
            pltpu.VMEM((fields, boxes) + box, f32),
            pltpu.VMEM((boxes, fields) + box, f32),
            pltpu.VMEM((boxes,) + box, f32),
            pltpu.VMEM((boxes, 3) + box, f32),
            halo,
            halo,
            halo,
            halo,
            pltpu.VMEM((2, 6, boxes) + box, f32),
            pltpu.VMEM((2, 6, 2, boxes, LANES), f32),
            pltpu.VMEM((2, boxes, LANES), f32),
            pltpu.VMEM((half, boxes) + box, f32),
            pltpu.VMEM((half, NONE + 1) + box, f32),
            pltpu.VMEM((half, homes) + box, f32),
            *slots,
            *slots,
            pltpu.VMEM((1, TABLE), I32),
            pltpu.SMEM((1, TABLE), I32),
            dma((4,)),
            dma((2, half + 1)),
            dma((2,)),
            dma((half,)),
            dma((1,)),
            dma((2,)),
            dma((2, half)),
            dma((4,)),
            dma((4, 2, half)),
        ],
        compiler_params=pltpu.CompilerParams(collective_id=0, has_side_effects=True, vmem_limit_bytes=38 << 20),
        name="regrid",
    )(new_owner.reshape(1, -1), new_owner, scale, state, kappa, flow)


def place_kernel(held, out, sem):
    parts = sem.shape[0]
    rows = held.shape[0] // parts
    copies = [
        pltpu.make_async_copy(held.at[pl.ds(i * rows, rows)], out.at[pl.ds(i * rows, rows)], sem.at[i])
        for i in range(parts)
    ]
    for copy in copies:
        copy.start()
    for copy in copies:
        copy.wait()


def placed(held):
    return pl.pallas_call(
        place_kernel,
        out_shape=pltpu.HBM(held.shape, held.dtype),
        in_specs=[pl.BlockSpec(memory_space=pltpu.VMEM)],
        out_specs=pl.BlockSpec(memory_space=pltpu.HBM),
        scratch_shapes=[pltpu.SemaphoreType.DMA((8,))],
        compiler_params=pltpu.CompilerParams(vmem_limit_bytes=12 << 20),
        name="placed",
    )(held)


def dense(result, new_owner):
    owners, here = lax.axis_size("bx"), lax.axis_index("bx")
    holding = result.shape[0]
    local_owner = lax.dynamic_slice_in_dim(new_owner, here * holding, holding)
    moving = local_owner != here
    targets = jnp.arange(owners, dtype=I32)
    picked = (local_owner[None, :] == targets[:, None]) & moving[None, :]
    source = jnp.sum(jnp.where(picked, jnp.arange(holding, dtype=I32)[None, :], 0), axis=1)
    present = jnp.any(picked, axis=1).reshape(owners, 1, 1, 1)
    chosen = lax.map(lambda i: lax.dynamic_index_in_dim(result, i, 0, keepdims=False), source)
    arrived = lax.all_to_all(jnp.where(present, chosen, 0.0), "bx", split_axis=0, concat_axis=0, tiled=True)
    staying = jnp.logical_not(moving).reshape(holding, 1, 1, 1)
    return jnp.concatenate([jnp.where(staying, result, 0.0), arrived], axis=0)


def on_device(state, diffusivity, velocity, species_scale, new_owner):
    inputs = (pltpu.with_memory_space_constraint(x[0], pltpu.HBM) for x in (state, diffusivity, velocity))
    held, res, lost = regrid(new_owner, species_scale, *inputs)
    out = placed(held).reshape((held.shape[0],) + state.shape[2:])
    return lax.fori_loop(0, lost[0], lambda _, out: dense(res, new_owner), out)[None]


def solution(mesh):
    in_specs = (
        P("xs", "bx", None, None, None),
        P("xs", "bx", None, None),
        P("xs", "bx", None, None, None),
        P(),
        P(),
    )
    out_specs = P("xs", "bx", None, None, None)
    return jax.shard_map(on_device, mesh=mesh, in_specs=in_specs, out_specs=out_specs, check_vma=False)
```

```python
import functools

import jax
import jax.numpy as jnp
from jax import lax
from jax.experimental import pallas as pl
from jax.experimental.pallas import tpu as pltpu
from jax.sharding import PartitionSpec as P

MESH = pl.DeviceIdType.MESH
time_step = 0.03
SIDE = 16
LANES = SIDE * SIDE


def moved(q, shift):
    return pltpu.roll(q, (-shift) % LANES, q.ndim - 1)


def update(q, behind, ahead, load, s):
    spread = None
    for n, other in enumerate(
        (behind, ahead, moved(q, -SIDE), moved(q, SIDE), moved(q, -1), moved(q, 1))
    ):
        a, b = load(n)
        term = (s * a + b) * (other - q)
        spread = term if spread is None else spread + term
    return q + spread


def weights(k, k_behind, k_ahead, u, v, w, store):
    lane = lax.broadcasted_iota(jnp.int32, k.shape, k.ndim - 1)
    y, z = lane // SIDE, lane % SIDE
    sides = (
        (k_behind, u, False, None),
        (k_ahead, u, True, None),
        (moved(k, -SIDE), v, False, y > 0),
        (moved(k, SIDE), v, True, y < SIDE - 1),
        (moved(k, -1), w, False, z > 0),
        (moved(k, 1), w, True, z < SIDE - 1),
    )
    for n, (other, speed, up, inside) in enumerate(sides):
        a = (0.5 * time_step) * (k + other)
        b = (-time_step) * jnp.minimum(speed, 0.0) if up else time_step * jnp.maximum(speed, 0.0)
        if inside is not None:
            a, b = jnp.where(inside, a, 0.0), jnp.where(inside, b, 0.0)
        store(n, a, b)


def joined(q, first, last):
    rows = q.shape[0]
    row = lax.broadcasted_iota(jnp.int32, q.shape, 0)
    behind = jnp.where(row == 0, jnp.broadcast_to(first, q.shape), pltpu.roll(q, 1, 0))
    ahead = jnp.where(row == rows - 1, jnp.broadcast_to(last, q.shape), pltpu.roll(q, rows - 1, 0))
    return behind, ahead


I32 = jnp.int32
CAPS = (6, 5, 10, 7)
LAGS = (0, 2, 4, 6, 8)
RING = 4
NODES = RING * RING
TABLE = 256
FINAL = 128
NONE = 16 + 2 * sum(CAPS)


def count(mask):
    return jnp.sum(jnp.where(mask, 1, 0), axis=0, keepdims=True)


def column(row):
    n = row.shape[1]
    eye = lax.broadcasted_iota(I32, (n, n), 0) == lax.broadcasted_iota(I32, (n, n), 1)
    return jnp.sum(jnp.where(eye, row, 0), axis=1, keepdims=True)


def node_values(values, at):
    across = lax.broadcasted_iota(I32, (NODES, 128), 0) == lax.broadcasted_iota(I32, (NODES, 128), 1)
    values = jnp.sum(jnp.where(across, values, 0), axis=1, keepdims=True)
    there = lax.broadcasted_iota(I32, (NODES, at.shape[1]), 0) == at
    return jnp.sum(jnp.where(there, values, 0), axis=0, keepdims=True)


def balanced(n1, n2, n3, most):
    up = lambda x: pltpu.roll(x, 128 - RING, 1)
    down = lambda x: pltpu.roll(x, RING, 1)
    place = lax.broadcasted_iota(I32, n1.shape, 1) // RING % 2
    within = lambda x: jnp.minimum(jnp.maximum(x, jnp.maximum(n2 - most, 0)), jnp.minimum(n2, most))
    half = within((n2 + n3 - n1 + 1) >> 1)
    for turn in (0, 1):
        rest = n2 - half
        with_up = jnp.maximum(n1 + down(half), up(n1) + up(half))
        with_down = jnp.maximum(n3 + up(rest), down(n3) + down(rest))
        half = jnp.where(place == turn, within((with_down + n2 - with_up + 1) >> 1), half)
    return half


def hops(at, d, first, second):
    n = at.shape[1]
    earlier = lax.broadcasted_iota(I32, (n, n), 0) < lax.broadcasted_iota(I32, (n, n), 1)
    at_c, d_c = column(at), column(d)
    r = count((at_c == at) & (d_c == d) & earlier)
    here = at_c == lax.broadcasted_iota(I32, (n, 128), 1) % NODES
    n1, n2, n3 = (count(here & (d_c == k)) for k in (1, 2, 3))
    half = balanced(n1, n2, n3, min(first, second))
    node_up, node_down = (at + RING) % NODES, (at + NODES - RING) % NODES
    ups, downs = node_values(half, at), node_values(n2 - half, at)
    two = d == 2
    up = jnp.where(two, jnp.where(r < ups, 1, 0), jnp.where(d == 1, 1, 0))
    rank = jnp.where(two, jnp.where(r < ups, r, r - ups), jnp.where(d == 1, ups + r, downs + r))
    mid = jnp.where(up == 1, node_up, node_down)
    local = jnp.where(up == 1, node_values(n1 + half, node_up), node_values(n3 + n2 - half, node_down))
    late = rank >= first
    slot = jnp.where(two, jnp.maximum(local - first, 0) + rank, rank - first)
    lost = (two & (late | (slot >= second))) | ((d > 0) & jnp.logical_not(two) & (slot >= second))
    return up, rank, late, slot, mid, jnp.sum(jnp.where(lost, 1, 0), keepdims=True)


def plan(owner, z, y, net):
    n = owner.shape[1]
    ka, kb, kc, kd = CAPS
    b = lax.broadcasted_iota(I32, owner.shape, 1)
    home = b // 8
    moving = owner != home

    def pq(chip):
        return (chip % RING, chip // RING) if net == 0 else (chip // RING, chip % RING)

    node = lambda p, q: p * RING + q
    p0, q0 = pq(home // 2)
    p1, q1 = pq(jnp.where(moving, owner, home) // 2)
    my_p, my_q = (y, z) if net == 0 else (z, y)
    me, me2 = node(my_p, my_q), node(my_q, my_p)
    turn = lambda p, k: (p + k) % RING
    base_a = 16
    base_b = base_a + 2 * ka
    base_c = base_b + 2 * kb
    base_d = base_c + 2 * kc
    own = b % 16
    d1 = turn(p1 - p0, RING)
    up1, rank1, late1, slot1, mid1, lost1 = hops(node(p0, q0), d1, ka, kb)
    in_a = base_a + (1 - up1) * ka + rank1
    at1 = jnp.where(d1 == 0, own, jnp.where((d1 == 2) | late1, base_b + (1 - up1) * kb + slot1, in_a))
    d2 = turn(q1 - q0, RING)
    up2, rank2, late2, slot2, mid2, lost2 = hops(node(q0, p1), d2, kc, kd)
    in_c = base_c + (1 - up2) * kc + rank2
    at2 = jnp.where(d2 == 0, at1, jnp.where((d2 == 2) | late2, base_d + (1 - up2) * kd + slot2, in_c))
    nodes = (node(p0, q0), node(q0, p1), node(q1, p1))
    entries = (
        ((nodes[0] == me) & (d1 > 0) & jnp.logical_not(late1), (1 - up1) * ka + rank1, own),
        ((nodes[0] == me) & (d1 > 0) & (d1 != 2) & late1, 2 * ka + (1 - up1) * kb + slot1, own),
        ((mid1 == me) & (d1 == 2), 2 * ka + (1 - up1) * kb + slot1, in_a),
        ((nodes[1] == me2) & (d2 > 0) & jnp.logical_not(late2), 2 * (ka + kb) + (1 - up2) * kc + rank2, at1),
        ((nodes[1] == me2) & (d2 > 0) & (d2 != 2) & late2, 2 * (ka + kb + kc) + (1 - up2) * kd + slot2, at1),
        ((mid2 == me2) & (d2 == 2), 2 * (ka + kb + kc) + (1 - up2) * kd + slot2, in_c),
        ((nodes[2] == me2) & moving, FINAL + (owner % 2) * 32 + home, at2 - NONE),
    )
    lane = lax.broadcasted_iota(I32, (n, TABLE), 1)
    table = jnp.where(lax.broadcasted_iota(I32, (1, TABLE), 1) >= FINAL, NONE, 0)
    for mask, slot, place in entries:
        slot, place = column(jnp.where(mask, slot, -1)), column(place)
        table = table + jnp.sum(jnp.where(lane == slot, place, 0), axis=0, keepdims=True)
    return jnp.clip(table, 0, NONE), lost1 + lost2


def both_plans(owner, z, y, core):
    one, lost_one = plan(owner, z, y, 0)
    two, lost_two = plan(owner, z, y, 1)
    row = jnp.where(core == 0, one, two)
    lane = lax.broadcasted_iota(I32, row.shape, 1)
    return jnp.where(lane == TABLE - 1, jnp.broadcast_to(jnp.minimum(lost_one + lost_two, 1), row.shape), row)


def regrid_kernel(
    fields, boxes, homes, owner_row, owner, scale, state_hbm, kappa_hbm, flow_hbm, out, res_hbm, lost,
    res, state, kappa, flow, up, down, low, high, wm, we, edge, sib, pool, fin, sa, sb, sc, sd, ra, rb, rc, rd,
    row, table, in_sem, halo_sem, halo_sent, sib_sem, sib_sent, fin_sem, keep_sem, send, recv,
):
    xs, bx, n_xs = lax.axis_index("xs"), lax.axis_index("bx"), lax.axis_size("xs")
    chip, core = bx // 2, bx % 2
    z, y = chip // RING, chip % RING
    half = fields // 2

    def device(dz, dy):
        return (xs, (((z + dz) % RING) * RING + (y + dy) % RING) * 2 + core)

    def peer(ring, step):
        along_y = (1 - core) if ring == 0 else core
        return device(step * (1 - along_y), step * along_y)

    sibling = (xs, bx + 1 - 2 * core)
    after, before = (lax.rem(xs + 1, n_xs), bx), (lax.rem(xs + n_xs - 1, n_xs), bx)
    around = [peer(ring, step) for ring in (0, 1) for step in (1, RING - 1)]
    barrier = pltpu.get_barrier_semaphore()
    for other in (after, before, sibling, *around):
        pl.semaphore_signal(barrier, inc=1, device_id=other, device_id_type=MESH)
    loads = [
        pltpu.make_async_copy(src, dst, in_sem.at[i])
        for i, (src, dst) in enumerate(((state_hbm, state), (kappa_hbm, kappa), (flow_hbm, flow)))
    ]
    for copy in loads:
        copy.start()
    for copy in loads:
        copy.wait()

    far_k, near_k, near_v = 2 * fields, 2 * fields + 1, 2 * fields + 2
    for buf, far, near in ((up, SIDE - 2, SIDE - 1), (down, 1, 0)):
        for b in range(boxes):
            one = pl.ds(b, 1)
            buf[far_k, one, :] = kappa[b, pl.ds(far, 1), :]
            buf[near_k, one, :] = kappa[b, pl.ds(near, 1), :]
            for d in range(3):
                buf[near_v + d, one, :] = flow[b, d, pl.ds(near, 1), :]

        @pl.loop(0, half)
        def _(t, buf=buf, far=far, near=near):
            for i in (0, 1):
                for side, row in enumerate((far, near)):
                    rows = [state[b, i * half + t, pl.ds(row, 1), :] for b in range(boxes)]
                    for b in range(boxes):
                        buf[4 * t + 2 * i + side, pl.ds(b, 1), :] = rows[b]

    pl.semaphore_wait(barrier, 3 + len(around))

    def ends_of(way, first, rows, part):
        src, dst, other = ((up, low, after), (down, high, before))[way]
        return pltpu.make_async_remote_copy(
            src_ref=src.at[pl.ds(first, rows)],
            dst_ref=dst.at[pl.ds(first, rows)],
            send_sem=halo_sent.at[way],
            recv_sem=halo_sem.at[way, part],
            device_id=other,
            device_id_type=MESH,
        )

    coefficients = [ends_of(way, far_k, 5, half) for way in (0, 1)]
    for copy in coefficients:
        copy.start()

    @pl.loop(0, half)
    def _(t):
        for way in (0, 1):
            ends_of(way, 4 * t, 4, t).start()

    row[...] = both_plans(owner_row[...], z, y, core)
    to_scalars = pltpu.make_async_copy(row, table, in_sem.at[3])
    to_scalars.start()
    for copy in coefficients:
        copy.wait_recv()

    def keep(ref, at):
        def store(n, a, b):
            ref[(0, n) + at] = a
            ref[(1, n) + at] = b

        return store

    for i, (far, near, own) in enumerate(((low, low, down), (high, high, up))):
        ends = (far[far_k], own[near_k])
        weights(near[near_k], *(ends if i == 0 else ends[::-1]), *(near[near_v + d] for d in range(3)), keep(we, (i,)))
    for b in range(boxes):
        k = kappa[b]
        behind, ahead = joined(k, low[near_k, pl.ds(b, 1), :], high[near_k, pl.ds(b, 1), :])
        weights(k, behind, ahead, flow[b, 0], flow[b, 1], flow[b, 2], keep(wm, (b,)))

    def advance(t, k):
        f = k * half + t
        s = scale[f]
        far, near = 4 * t + 2 * k, 4 * t + 2 * k + 1
        for i, (halo, own) in enumerate(((low, down), (high, up))):
            ends = (halo[far], own[near])
            edge[i] = update(halo[near], *(ends if i == 0 else ends[::-1]), lambda n: (we[0, n, i], we[1, n, i]), s)
        for b in range(boxes):
            load = lambda n: (wm[0, n, b], wm[1, n, b])
            one = pl.ds(b, 1)
            q = state[b, f]
            q = update(q, *joined(q, low[near, one, :], high[near, one, :]), load, s)
            q = update(q, *joined(q, edge[0, one, :], edge[1, one, :]), load, s)
            res[f, b] = q
            out[b, k, t] = jnp.where(owner[bx * boxes + b] == bx, q, 0.0)

    def to_sibling(src, dst, t):
        return pltpu.make_async_remote_copy(
            src_ref=src, dst_ref=dst, send_sem=sib_sent.at[0], recv_sem=sib_sem.at[t], device_id=sibling, device_id_type=MESH
        )

    def share(t):
        return to_sibling(res.at[(1 - core) * half + t], sib.at[t], t)

    def back(src, dst):
        return pltpu.make_async_remote_copy(
            src_ref=src, dst_ref=dst, send_sem=fin_sem.at[0], recv_sem=fin_sem.at[1], device_id=sibling, device_id_type=MESH
        )

    def kept(k, t):
        return pltpu.make_async_copy(res.at[k * half + t], res_hbm.at[:, k * half + t], keep_sem.at[k, t])

    outgoing, incoming = (sa, sb, sc, sd), (ra, rb, rc, rd)
    start = [2 * sum(CAPS[:i]) for i in range(4)]

    def hop(stage, way, t):
        return pltpu.make_async_remote_copy(
            src_ref=outgoing[stage].at[t, way],
            dst_ref=incoming[stage].at[t, way],
            send_sem=send.at[stage],
            recv_sem=recv.at[stage, way, t],
            device_id=around[(stage // 2) * 2 + way],
            device_id_type=MESH,
        )

    def compute(t):
        for way in (0, 1):
            ends_of(way, 4 * t, 4, t).wait_recv()

        @pl.loop(0, 2)
        def _(k):
            advance(t, k)

        share(t).start()
        kept(0, t).start()
        kept(1, t).start()

    def pick(t, first, places, store):
        for k in range(0, places, 6):
            group = range(k, min(k + 6, places))
            values = [pool[t, table[0, first + j]] for j in group]
            for j, value in zip(group, values):
                store(j, value)

    def gather(stage, t):
        slots = CAPS[stage]
        for way in (0, 1):

            def store(k, value, way=way):
                outgoing[stage][t, way, k] = value

            pick(t, start[stage] + way * slots, slots, store)
            hop(stage, way, t).start()

    def take(stage, t):
        for way in (0, 1):
            hop(stage, way, t).wait_recv()
            pool[t, pl.ds(16 + start[stage] + way * CAPS[stage], CAPS[stage])] = incoming[stage][t, way]

    def first(t):
        share(t).wait_recv()
        pool[t, pl.ds(core * boxes, boxes)] = res[core * half + t]
        pool[t, pl.ds((1 - core) * boxes, boxes)] = sib[t]
        pool[t, NONE] = jnp.zeros((SIDE, LANES), jnp.float32)
        gather(0, t)

    def middle(stage):
        def run(t):
            take(stage - 1, t)
            gather(stage, t)

        return run

    def last(t):
        take(3, t)

        def store_far(h, value):
            fin[t, h] = value

        def store_near(h, value):
            out[boxes + h, core, t] = value

        pick(t, FINAL + (1 - core) * 32, homes, store_far)
        back(fin.at[t], out.at[pl.ds(boxes, homes), core, t]).start()
        pick(t, FINAL + core * 32, homes, store_near)

    steps = (first, middle(1), middle(2), middle(3), last)
    compute(0)
    compute(1)
    to_scalars.wait()
    lost[0] = table[0, TABLE - 1]

    @pl.loop(0, half + LAGS[-1])
    def _(t):
        for lag, run in zip(LAGS, steps):

            @pl.when((t >= lag) & (t < half + lag))
            def _(run=run, lag=lag):
                run(t - lag)

        @pl.when(t + 2 < half)
        def _():
            compute(t + 2)

    for way, (src, other) in enumerate(((up, after), (down, before))):
        pltpu.make_async_remote_copy(
            src_ref=src,
            dst_ref=src,
            send_sem=halo_sent.at[way],
            recv_sem=halo_sem.at[way, 0],
            device_id=other,
            device_id_type=MESH,
        ).wait_send()
    to_sibling(sib, sib, 0).wait_send()
    back(fin, fin).wait()
    for stage in range(4):
        pltpu.make_async_remote_copy(
            src_ref=outgoing[stage],
            dst_ref=incoming[stage],
            send_sem=send.at[stage],
            recv_sem=recv.at[stage, 0, 0],
            device_id=sibling,
            device_id_type=MESH,
        ).wait_send()

    @pl.loop(0, half)
    def _(t):
        for k in (0, 1):
            kept(k, t).wait()


def regrid(new_owner, scale, state, kappa, flow):
    boxes, fields = state.shape[:2]
    homes = new_owner.shape[0] // boxes
    half = fields // 2
    f32 = jnp.float32
    vmem, smem, hbm = (pl.BlockSpec(memory_space=m) for m in (pltpu.VMEM, pltpu.SMEM, pltpu.HBM))
    box = (SIDE, LANES)
    halo = pltpu.VMEM((2 * fields + 5, boxes, LANES), f32)
    slots = [pltpu.VMEM((half, 2, k) + box, f32) for k in CAPS]
    dma = pltpu.SemaphoreType.DMA
    return pl.pallas_call(
        functools.partial(regrid_kernel, fields, boxes, homes),
        out_shape=[
            pltpu.VMEM((boxes + homes, 2, half) + box, f32),
            pltpu.HBM((boxes, fields) + box, f32),
            jax.ShapeDtypeStruct((1,), I32),
        ],
        in_specs=[vmem, smem, smem, hbm, hbm, hbm],
        out_specs=[vmem, hbm, smem],
        scratch_shapes=[
            pltpu.VMEM((fields, boxes) + box, f32),
            pltpu.VMEM((boxes, fields) + box, f32),
            pltpu.VMEM((boxes,) + box, f32),
            pltpu.VMEM((boxes, 3) + box, f32),
            halo,
            halo,
            halo,
            halo,
            pltpu.VMEM((2, 6, boxes) + box, f32),
            pltpu.VMEM((2, 6, 2, boxes, LANES), f32),
            pltpu.VMEM((2, boxes, LANES), f32),
            pltpu.VMEM((half, boxes) + box, f32),
            pltpu.VMEM((half, NONE + 1) + box, f32),
            pltpu.VMEM((half, homes) + box, f32),
            *slots,
            *slots,
            pltpu.VMEM((1, TABLE), I32),
            pltpu.SMEM((1, TABLE), I32),
            dma((4,)),
            dma((2, half + 1)),
            dma((2,)),
            dma((half,)),
            dma((1,)),
            dma((2,)),
            dma((2, half)),
            dma((4,)),
            dma((4, 2, half)),
        ],
        compiler_params=pltpu.CompilerParams(collective_id=0, has_side_effects=True, vmem_limit_bytes=38 << 20),
        name="regrid",
    )(new_owner.reshape(1, -1), new_owner, scale, state, kappa, flow)


def place_kernel(held, out, sem):
    parts = sem.shape[0]
    rows = held.shape[0] // parts
    copies = [
        pltpu.make_async_copy(held.at[pl.ds(i * rows, rows)], out.at[pl.ds(i * rows, rows)], sem.at[i])
        for i in range(parts)
    ]
    for copy in copies:
        copy.start()
    for copy in copies:
        copy.wait()


def placed(held):
    return pl.pallas_call(
        place_kernel,
        out_shape=pltpu.HBM(held.shape, held.dtype),
        in_specs=[pl.BlockSpec(memory_space=pltpu.VMEM)],
        out_specs=pl.BlockSpec(memory_space=pltpu.HBM),
        scratch_shapes=[pltpu.SemaphoreType.DMA((8,))],
        compiler_params=pltpu.CompilerParams(vmem_limit_bytes=12 << 20),
        name="placed",
    )(held)


def dense(result, new_owner):
    owners, here = lax.axis_size("bx"), lax.axis_index("bx")
    holding = result.shape[0]
    local_owner = lax.dynamic_slice_in_dim(new_owner, here * holding, holding)
    moving = local_owner != here
    targets = jnp.arange(owners, dtype=I32)
    picked = (local_owner[None, :] == targets[:, None]) & moving[None, :]
    source = jnp.sum(jnp.where(picked, jnp.arange(holding, dtype=I32)[None, :], 0), axis=1)
    present = jnp.any(picked, axis=1).reshape(owners, 1, 1, 1)
    chosen = lax.map(lambda i: lax.dynamic_index_in_dim(result, i, 0, keepdims=False), source)
    arrived = lax.all_to_all(jnp.where(present, chosen, 0.0), "bx", split_axis=0, concat_axis=0, tiled=True)
    staying = jnp.logical_not(moving).reshape(holding, 1, 1, 1)
    return jnp.concatenate([jnp.where(staying, result, 0.0), arrived], axis=0)


def on_device(state, diffusivity, velocity, species_scale, new_owner):
    inputs = (pltpu.with_memory_space_constraint(x[0], pltpu.HBM) for x in (state, diffusivity, velocity))
    held, res, lost = regrid(new_owner, species_scale, *inputs)
    out = placed(held).reshape((held.shape[0],) + state.shape[2:])
    return lax.fori_loop(0, lost[0], lambda _, out: dense(res, new_owner), out)[None]


def solution(mesh):
    in_specs = (
        P("xs", "bx", None, None, None),
        P("xs", "bx", None, None),
        P("xs", "bx", None, None, None),
        P(),
        P(),
    )
    out_specs = P("xs", "bx", None, None, None)
    return jax.shard_map(on_device, mesh=mesh, in_specs=in_specs, out_specs=out_specs, check_vma=False)
```

```python
import functools

import jax
import jax.numpy as jnp
from jax import lax
from jax.experimental import pallas as pl
from jax.experimental.pallas import tpu as pltpu
from jax.sharding import PartitionSpec as P

MESH = pl.DeviceIdType.MESH
time_step = 0.03
SIDE = 16
LANES = SIDE * SIDE


def moved(q, shift):
    return pltpu.roll(q, (-shift) % LANES, q.ndim - 1)


def update(q, behind, ahead, load, s):
    spread = None
    for n, other in enumerate(
        (behind, ahead, moved(q, -SIDE), moved(q, SIDE), moved(q, -1), moved(q, 1))
    ):
        a, b = load(n)
        term = (s * a + b) * (other - q)
        spread = term if spread is None else spread + term
    return q + spread


def weight(k, other, speed, up, inside=None):
    a = (0.5 * time_step) * (k + other)
    b = (-time_step) * jnp.minimum(speed, 0.0) if up else time_step * jnp.maximum(speed, 0.0)
    if inside is not None:
        a, b = jnp.where(inside, a, 0.0), jnp.where(inside, b, 0.0)
    return a, b


def weights_x(k, k_behind, k_ahead, u, store):
    for n, other in enumerate((k_behind, k_ahead)):
        store(n, *weight(k, other, u, n == 1))


def weights_yz(k, v, w, store):
    lane = lax.broadcasted_iota(jnp.int32, k.shape, k.ndim - 1)
    y, z = lane // SIDE, lane % SIDE
    sides = ((-SIDE, v, y > 0), (SIDE, v, y < SIDE - 1), (-1, w, z > 0), (1, w, z < SIDE - 1))
    for n, (shift, speed, inside) in enumerate(sides):
        store(2 + n, *weight(k, moved(k, shift), speed, shift > 0, inside))


def joined(q, first, last):
    rows = q.shape[0]
    row = lax.broadcasted_iota(jnp.int32, q.shape, 0)
    behind = jnp.where(row == 0, jnp.broadcast_to(first, q.shape), pltpu.roll(q, 1, 0))
    ahead = jnp.where(row == rows - 1, jnp.broadcast_to(last, q.shape), pltpu.roll(q, rows - 1, 0))
    return behind, ahead


I32 = jnp.int32
CAPS = (6, 5, 10, 7)
LAGS = (0, 2, 4, 6, 8)
PIECES = 1
ROWS = SIDE // PIECES
RING = 4
NODES = RING * RING
TABLE = 256
FINAL = 128
NONE = 16 + 2 * sum(CAPS)


def count(mask):
    return jnp.sum(jnp.where(mask, 1, 0), axis=0, keepdims=True)


def column(row):
    n = row.shape[1]
    eye = lax.broadcasted_iota(I32, (n, n), 0) == lax.broadcasted_iota(I32, (n, n), 1)
    return jnp.sum(jnp.where(eye, row, 0), axis=1, keepdims=True)


def node_values(values, at):
    across = lax.broadcasted_iota(I32, (NODES, 128), 0) == lax.broadcasted_iota(I32, (NODES, 128), 1)
    values = jnp.sum(jnp.where(across, values, 0), axis=1, keepdims=True)
    there = lax.broadcasted_iota(I32, (NODES, at.shape[1]), 0) == at
    return jnp.sum(jnp.where(there, values, 0), axis=0, keepdims=True)


def balanced(n1, n2, n3, most):
    up = lambda x: pltpu.roll(x, 128 - RING, 1)
    down = lambda x: pltpu.roll(x, RING, 1)
    place = lax.broadcasted_iota(I32, n1.shape, 1) // RING % 2
    within = lambda x: jnp.minimum(jnp.maximum(x, jnp.maximum(n2 - most, 0)), jnp.minimum(n2, most))
    half = within((n2 + n3 - n1 + 1) >> 1)
    for turn in (0, 1):
        rest = n2 - half
        with_up = jnp.maximum(n1 + down(half), up(n1) + up(half))
        with_down = jnp.maximum(n3 + up(rest), down(n3) + down(rest))
        half = jnp.where(place == turn, within((with_down + n2 - with_up + 1) >> 1), half)
    return half


def hops(at, d, first, second):
    n = at.shape[1]
    earlier = lax.broadcasted_iota(I32, (n, n), 0) < lax.broadcasted_iota(I32, (n, n), 1)
    at_c, d_c = column(at), column(d)
    r = count((at_c == at) & (d_c == d) & earlier)
    here = at_c == lax.broadcasted_iota(I32, (n, 128), 1) % NODES
    n1, n2, n3 = (count(here & (d_c == k)) for k in (1, 2, 3))
    half = balanced(n1, n2, n3, min(first, second))
    node_up, node_down = (at + RING) % NODES, (at + NODES - RING) % NODES
    ups, downs = node_values(half, at), node_values(n2 - half, at)
    two = d == 2
    up = jnp.where(two, jnp.where(r < ups, 1, 0), jnp.where(d == 1, 1, 0))
    rank = jnp.where(two, jnp.where(r < ups, r, r - ups), jnp.where(d == 1, ups + r, downs + r))
    mid = jnp.where(up == 1, node_up, node_down)
    local = jnp.where(up == 1, node_values(n1 + half, node_up), node_values(n3 + n2 - half, node_down))
    late = rank >= first
    slot = jnp.where(two, jnp.maximum(local - first, 0) + rank, rank - first)
    lost = (two & (late | (slot >= second))) | ((d > 0) & jnp.logical_not(two) & (slot >= second))
    return up, rank, late, slot, mid, jnp.sum(jnp.where(lost, 1, 0), keepdims=True)


def plan(owner, z, y, net):
    ka, kb, kc, kd = CAPS
    b = lax.broadcasted_iota(I32, owner.shape, 1)
    home = b // 8
    moving = owner != home

    def pq(chip):
        return (chip % RING, chip // RING) if net == 0 else (chip // RING, chip % RING)

    node = lambda p, q: p * RING + q
    p0, q0 = pq(home // 2)
    p1, q1 = pq(jnp.where(moving, owner, home) // 2)
    my_p, my_q = (y, z) if net == 0 else (z, y)
    me, me2 = node(my_p, my_q), node(my_q, my_p)
    turn = lambda p, k: (p + k) % RING
    base_a = 16
    base_b = base_a + 2 * ka
    base_c = base_b + 2 * kb
    base_d = base_c + 2 * kc
    own = b % 16
    d1 = turn(p1 - p0, RING)
    up1, rank1, late1, slot1, mid1, lost1 = hops(node(p0, q0), d1, ka, kb)
    in_a = base_a + (1 - up1) * ka + rank1
    at1 = jnp.where(d1 == 0, own, jnp.where((d1 == 2) | late1, base_b + (1 - up1) * kb + slot1, in_a))
    d2 = turn(q1 - q0, RING)
    up2, rank2, late2, slot2, mid2, lost2 = hops(node(q0, p1), d2, kc, kd)
    in_c = base_c + (1 - up2) * kc + rank2
    at2 = jnp.where(d2 == 0, at1, jnp.where((d2 == 2) | late2, base_d + (1 - up2) * kd + slot2, in_c))
    nodes = (node(p0, q0), node(q0, p1), node(q1, p1))
    entries = (
        ((nodes[0] == me) & (d1 > 0) & jnp.logical_not(late1), (1 - up1) * ka + rank1, own),
        ((nodes[0] == me) & (d1 > 0) & (d1 != 2) & late1, 2 * ka + (1 - up1) * kb + slot1, own),
        ((mid1 == me) & (d1 == 2), 2 * ka + (1 - up1) * kb + slot1, in_a),
        ((nodes[1] == me2) & (d2 > 0) & jnp.logical_not(late2), 2 * (ka + kb) + (1 - up2) * kc + rank2, at1),
        ((nodes[1] == me2) & (d2 > 0) & (d2 != 2) & late2, 2 * (ka + kb + kc) + (1 - up2) * kd + slot2, at1),
        ((mid2 == me2) & (d2 == 2), 2 * (ka + kb + kc) + (1 - up2) * kd + slot2, in_c),
        ((nodes[2] == me2) & moving, FINAL + (owner % 2) * 32 + home, at2 - NONE),
    )
    return [(jnp.where(mask, slot, -1), place) for mask, slot, place in entries], lost1 + lost2


def both_plans(owner, z, y, core):
    n = owner.shape[1]
    one, lost_one = plan(owner, z, y, 0)
    two, lost_two = plan(owner, z, y, 1)
    number = lax.broadcasted_iota(I32, (TABLE, n), 0)
    table = jnp.zeros((TABLE, n), I32)
    for (slot_one, place_one), (slot_two, place_two) in zip(one, two):
        slot, place = jnp.where(core == 0, slot_one, slot_two), jnp.where(core == 0, place_one, place_two)
        table = table + jnp.where(number == slot, place, 0)
    table = jnp.sum(table, axis=1, keepdims=True)
    eye = lax.broadcasted_iota(I32, (TABLE, TABLE), 0) == lax.broadcasted_iota(I32, (TABLE, TABLE), 1)
    row = jnp.sum(jnp.where(eye, table, 0), axis=0, keepdims=True)
    lane = lax.broadcasted_iota(I32, row.shape, 1)
    row = jnp.clip(row + jnp.where(lane >= FINAL, NONE, 0), 0, NONE)
    return jnp.where(lane == TABLE - 1, jnp.broadcast_to(jnp.minimum(lost_one + lost_two, 1), row.shape), row)


def regrid_kernel(
    fields, boxes, homes, owner_row, owner_hbm, scale_hbm, state_hbm, kappa_hbm, flow_hbm, out, res_hbm, lost,
    res, state, kappa, flow, up, down, low, high, wm, we, edge, sib, pool, fin, sa, sb, sc, sd, ra, rb, rc, rd,
    row, table, owner, scale, in_sem, halo_sem, halo_sent, sib_sem, sib_sent, fin_sem, keep_sem, send, recv,
):
    xs, bx, n_xs = lax.axis_index("xs"), lax.axis_index("bx"), lax.axis_size("xs")
    chip, core = bx // 2, bx % 2
    z, y = chip // RING, chip % RING
    half = fields // 2

    def device(dz, dy):
        return (xs, (((z + dz) % RING) * RING + (y + dy) % RING) * 2 + core)

    def peer(ring, step):
        along_y = (1 - core) if ring == 0 else core
        return device(step * (1 - along_y), step * along_y)

    sibling = (xs, bx + 1 - 2 * core)
    after, before = (lax.rem(xs + 1, n_xs), bx), (lax.rem(xs + n_xs - 1, n_xs), bx)
    around = [peer(ring, step) for ring in (0, 1) for step in (1, RING - 1)]
    barrier = pltpu.get_barrier_semaphore()
    for other in (after, before, sibling, *around):
        pl.semaphore_signal(barrier, inc=1, device_id=other, device_id_type=MESH)
    loads = [
        pltpu.make_async_copy(src, dst, in_sem.at[i])
        for i, (src, dst) in enumerate(
            ((state_hbm, state), (kappa_hbm, kappa), (flow_hbm, flow), (owner_hbm, owner), (scale_hbm, scale))
        )
    ]
    for copy in loads:
        copy.start()
    for copy in loads:
        copy.wait()

    far_k, near_k, near_v = 2 * fields, 2 * fields + 1, 2 * fields + 2
    for buf, far, near in ((up, SIDE - 2, SIDE - 1), (down, 1, 0)):
        for b in range(boxes):
            one = pl.ds(b, 1)
            buf[far_k, one, :] = kappa[b, pl.ds(far, 1), :]
            buf[near_k, one, :] = kappa[b, pl.ds(near, 1), :]
            for d in range(3):
                buf[near_v + d, one, :] = flow[b, d, pl.ds(near, 1), :]

        @pl.loop(0, half)
        def _(t, buf=buf, far=far, near=near):
            for i in (0, 1):
                for side, row in enumerate((far, near)):
                    rows = [state[b, i * half + t, pl.ds(row, 1), :] for b in range(boxes)]
                    for b in range(boxes):
                        buf[4 * t + 2 * i + side, pl.ds(b, 1), :] = rows[b]

    pl.semaphore_wait(barrier, 3 + len(around))

    def ends_of(way, first, rows, part):
        src, dst, other = ((up, low, after), (down, high, before))[way]
        return pltpu.make_async_remote_copy(
            src_ref=src.at[pl.ds(first, rows)],
            dst_ref=dst.at[pl.ds(first, rows)],
            send_sem=halo_sent.at[way],
            recv_sem=halo_sem.at[way, part],
            device_id=other,
            device_id_type=MESH,
        )

    coefficients = [ends_of(way, far_k, 5, half) for way in (0, 1)]
    for copy in coefficients:
        copy.start()

    def send_ends(t):
        for way in (0, 1):
            ends_of(way, 4 * t, 4, t).start()

    send_ends(0)
    send_ends(1)
    def keep(ref, at):
        def store(n, a, b):
            ref[(0, n) + at] = a
            ref[(1, n) + at] = b

        return store

    row[...] = both_plans(owner_row[...], z, y, core)
    to_scalars = pltpu.make_async_copy(row, table, in_sem.at[5])
    to_scalars.start()
    for b in range(boxes):
        weights_yz(kappa[b], flow[b, 1], flow[b, 2], keep(wm, (b,)))
    for copy in coefficients:
        copy.wait_recv()

    @pl.loop(2, half)
    def _(t):
        send_ends(t)

    for i, (halo, own) in enumerate(((low, down), (high, up))):
        k, ends = halo[near_k], (halo[far_k], own[near_k])
        weights_x(k, *(ends if i == 0 else ends[::-1]), halo[near_v], keep(we, (i,)))
        weights_yz(k, halo[near_v + 1], halo[near_v + 2], keep(we, (i,)))
    for b in range(boxes):
        k = kappa[b]
        behind, ahead = joined(k, low[near_k, pl.ds(b, 1), :], high[near_k, pl.ds(b, 1), :])
        weights_x(k, behind, ahead, flow[b, 0], keep(wm, (b,)))

    def advance(t, k):
        f = k * half + t
        s = scale[f]
        far, near = 4 * t + 2 * k, 4 * t + 2 * k + 1
        for i, (halo, own) in enumerate(((low, down), (high, up))):
            ends = (halo[far], own[near])
            edge[i] = update(halo[near], *(ends if i == 0 else ends[::-1]), lambda n: (we[0, n, i], we[1, n, i]), s)
        for b in range(boxes):
            load = lambda n: (wm[0, n, b], wm[1, n, b])
            one = pl.ds(b, 1)
            q = state[b, f]
            q = update(q, *joined(q, low[near, one, :], high[near, one, :]), load, s)
            q = update(q, *joined(q, edge[0, one, :], edge[1, one, :]), load, s)
            res[f, b] = q
            out[b, k, t] = jnp.where(owner[bx * boxes + b] == bx, q, 0.0)

    def to_sibling(src, dst, t):
        return pltpu.make_async_remote_copy(
            src_ref=src, dst_ref=dst, send_sem=sib_sent.at[0], recv_sem=sib_sem.at[t], device_id=sibling, device_id_type=MESH
        )

    def rows_of(part):
        return part // PIECES, pl.ds(pl.multiple_of(part % PIECES * ROWS, ROWS), ROWS)

    def share(part):
        t, rows = rows_of(part)
        return to_sibling(res.at[(1 - core) * half + t, :, rows], sib.at[part], part)

    def back(src, dst):
        return pltpu.make_async_remote_copy(
            src_ref=src, dst_ref=dst, send_sem=fin_sem.at[0], recv_sem=fin_sem.at[1], device_id=sibling, device_id_type=MESH
        )

    def kept(k, t):
        return pltpu.make_async_copy(res.at[k * half + t], res_hbm.at[:, k * half + t], keep_sem.at[k, t])

    outgoing, incoming = (sa, sb, sc, sd), (ra, rb, rc, rd)
    start = [2 * sum(CAPS[:i]) for i in range(4)]

    def hop(stage, way, t):
        return pltpu.make_async_remote_copy(
            src_ref=outgoing[stage].at[t, way],
            dst_ref=incoming[stage].at[t, way],
            send_sem=send.at[stage],
            recv_sem=recv.at[stage, way, t],
            device_id=around[(stage // 2) * 2 + way],
            device_id_type=MESH,
        )

    def compute(t):
        for way in (0, 1):
            ends_of(way, 4 * t, 4, t).wait_recv()

        @pl.loop(0, 2)
        def _(k):
            advance(t, k)

        for piece in range(PIECES):
            share(t * PIECES + piece).start()
        kept(0, t).start()
        kept(1, t).start()

    def pick(t, first, places, store):
        for k in range(0, places, 6 * PIECES):
            group = range(k, min(k + 6 * PIECES, places))
            values = [pool[t, table[0, first + j]] for j in group]
            for j, value in zip(group, values):
                store(j, value)

    def gather(stage, t):
        slots = CAPS[stage]
        for way in (0, 1):

            def store(k, value, way=way):
                outgoing[stage][t, way, k] = value

            pick(t, start[stage] + way * slots, slots, store)
            hop(stage, way, t).start()

    def take(stage, t):
        for way in (0, 1):
            hop(stage, way, t).wait_recv()
            pool[t, pl.ds(16 + start[stage] + way * CAPS[stage], CAPS[stage])] = incoming[stage][t, way]

    def first(part):
        share(part).wait_recv()
        t, rows = rows_of(part)
        pool[part, pl.ds(core * boxes, boxes)] = res[core * half + t, :, rows]
        pool[part, pl.ds((1 - core) * boxes, boxes)] = sib[part]
        pool[part, NONE] = jnp.zeros((ROWS, LANES), jnp.float32)
        gather(0, part)

    def middle(stage):
        def run(t):
            take(stage - 1, t)
            gather(stage, t)

        return run

    def last(part):
        take(3, part)
        t, rows = rows_of(part)

        def store_far(h, value):
            fin[part, h] = value

        def store_near(h, value):
            out[boxes + h, core, t, rows] = value

        pick(part, FINAL + (1 - core) * 32, homes, store_far)
        back(fin.at[part], out.at[pl.ds(boxes, homes), core, t, rows]).start()
        pick(part, FINAL + core * 32, homes, store_near)

    steps = (first, middle(1), middle(2), middle(3), last)
    compute(0)
    compute(1)
    to_scalars.wait()
    lost[0] = table[0, TABLE - 1]

    parts = half * PIECES

    @pl.loop(0, parts + LAGS[-1])
    def _(t):
        for lag, run in zip(LAGS, steps):

            @pl.when((t >= lag) & (t < parts + lag))
            def _(run=run, lag=lag):
                run(t - lag)

        @pl.when((t % PIECES == 0) & (t // PIECES + 2 < half))
        def _():
            compute(t // PIECES + 2)

    for way, (src, other) in enumerate(((up, after), (down, before))):
        pltpu.make_async_remote_copy(
            src_ref=src,
            dst_ref=src,
            send_sem=halo_sent.at[way],
            recv_sem=halo_sem.at[way, 0],
            device_id=other,
            device_id_type=MESH,
        ).wait_send()
    to_sibling(sib, sib, 0).wait_send()
    back(fin, fin).wait()
    for stage in range(4):
        pltpu.make_async_remote_copy(
            src_ref=outgoing[stage],
            dst_ref=incoming[stage],
            send_sem=send.at[stage],
            recv_sem=recv.at[stage, 0, 0],
            device_id=sibling,
            device_id_type=MESH,
        ).wait_send()

    @pl.loop(0, half)
    def _(t):
        for k in (0, 1):
            kept(k, t).wait()


def regrid(owner_row, new_owner, scale, state, kappa, flow):
    boxes, fields = state.shape[:2]
    homes = new_owner.shape[0] // boxes
    half = fields // 2
    f32 = jnp.float32
    vmem, smem, hbm = (pl.BlockSpec(memory_space=m) for m in (pltpu.VMEM, pltpu.SMEM, pltpu.HBM))
    box = (SIDE, LANES)
    halo = pltpu.VMEM((2 * fields + 5, boxes, LANES), f32)
    parts, piece = half * PIECES, (ROWS, LANES)
    slots = [pltpu.VMEM((parts, 2, k) + piece, f32) for k in CAPS]
    dma = pltpu.SemaphoreType.DMA
    return pl.pallas_call(
        functools.partial(regrid_kernel, fields, boxes, homes),
        out_shape=[
            pltpu.VMEM((boxes + homes, 2, half) + box, f32),
            pltpu.HBM((boxes, fields) + box, f32),
            jax.ShapeDtypeStruct((1,), I32),
        ],
        in_specs=[vmem, hbm, hbm, hbm, hbm, hbm],
        out_specs=[vmem, hbm, smem],
        scratch_shapes=[
            pltpu.VMEM((fields, boxes) + box, f32),
            pltpu.VMEM((boxes, fields) + box, f32),
            pltpu.VMEM((boxes,) + box, f32),
            pltpu.VMEM((boxes, 3) + box, f32),
            halo,
            halo,
            halo,
            halo,
            pltpu.VMEM((2, 6, boxes) + box, f32),
            pltpu.VMEM((2, 6, 2, boxes, LANES), f32),
            pltpu.VMEM((2, boxes, LANES), f32),
            pltpu.VMEM((parts, boxes) + piece, f32),
            pltpu.VMEM((parts, NONE + 1) + piece, f32),
            pltpu.VMEM((parts, homes) + piece, f32),
            *slots,
            *slots,
            pltpu.VMEM((1, TABLE), I32),
            pltpu.SMEM((1, TABLE), I32),
            pltpu.SMEM(new_owner.shape, I32),
            pltpu.SMEM(scale.shape, f32),
            dma((6,)),
            dma((2, half + 1)),
            dma((2,)),
            dma((parts,)),
            dma((1,)),
            dma((2,)),
            dma((2, half)),
            dma((4,)),
            dma((4, 2, parts)),
        ],
        compiler_params=pltpu.CompilerParams(collective_id=0, has_side_effects=True, vmem_limit_bytes=38 << 20),
        name="regrid",
    )(owner_row, new_owner, scale, state, kappa, flow)


def place_kernel(held, out, sem):
    parts = sem.shape[0]
    rows = held.shape[0] // parts
    copies = [
        pltpu.make_async_copy(held.at[pl.ds(i * rows, rows)], out.at[pl.ds(i * rows, rows)], sem.at[i])
        for i in range(parts)
    ]
    for copy in copies:
        copy.start()
    for copy in copies:
        copy.wait()


def placed(held):
    return pl.pallas_call(
        place_kernel,
        out_shape=pltpu.HBM(held.shape, held.dtype),
        in_specs=[pl.BlockSpec(memory_space=pltpu.VMEM)],
        out_specs=pl.BlockSpec(memory_space=pltpu.HBM),
        scratch_shapes=[pltpu.SemaphoreType.DMA((8,))],
        compiler_params=pltpu.CompilerParams(vmem_limit_bytes=12 << 20),
        name="placed",
    )(held)


def dense(result, new_owner):
    owners, here = lax.axis_size("bx"), lax.axis_index("bx")
    holding = result.shape[0]
    local_owner = lax.dynamic_slice_in_dim(new_owner, here * holding, holding)
    moving = local_owner != here
    targets = jnp.arange(owners, dtype=I32)
    picked = (local_owner[None, :] == targets[:, None]) & moving[None, :]
    source = jnp.sum(jnp.where(picked, jnp.arange(holding, dtype=I32)[None, :], 0), axis=1)
    present = jnp.any(picked, axis=1).reshape(owners, 1, 1, 1)
    chosen = result[:1]
    for b in range(1, holding):
        chosen = jnp.where((source == b).reshape(owners, 1, 1, 1), result[b], chosen)
    arrived = lax.all_to_all(jnp.where(present, chosen, 0.0), "bx", split_axis=0, concat_axis=0, tiled=True)
    staying = jnp.logical_not(moving).reshape(holding, 1, 1, 1)
    return jnp.concatenate([jnp.where(staying, result, 0.0), arrived], axis=0)


def on_device(state, diffusivity, velocity, species_scale, new_owner):
    inputs = (
        pltpu.with_memory_space_constraint(x, pltpu.HBM)
        for x in (new_owner, species_scale, state[0], diffusivity[0], velocity[0])
    )
    held, res, lost = regrid(new_owner.reshape(1, -1), *inputs)
    out = placed(held).reshape((held.shape[0],) + state.shape[2:])

    def again(i, out):
        _, owner = lax.optimization_barrier((i, new_owner))
        return dense(res, owner)

    return lax.fori_loop(0, lost[0], again, out)[None]


def solution(mesh):
    in_specs = (
        P("xs", "bx", None, None, None),
        P("xs", "bx", None, None),
        P("xs", "bx", None, None, None),
        P(),
        P(),
    )
    out_specs = P("xs", "bx", None, None, None)
    return jax.shard_map(on_device, mesh=mesh, in_specs=in_specs, out_specs=out_specs, check_vma=False)
```

```python
import functools

import jax
import jax.numpy as jnp
from jax import lax
from jax.experimental import pallas as pl
from jax.experimental.pallas import tpu as pltpu
from jax.sharding import PartitionSpec as P

MESH = pl.DeviceIdType.MESH
time_step = 0.03
SIDE = 16
LANES = SIDE * SIDE


def moved(q, shift):
    return pltpu.roll(q, (-shift) % LANES, q.ndim - 1)


def update(q, behind, ahead, load, s):
    spread = None
    for n, other in enumerate(
        (behind, ahead, moved(q, -SIDE), moved(q, SIDE), moved(q, -1), moved(q, 1))
    ):
        a, b = load(n)
        term = (s * a + b) * (other - q)
        spread = term if spread is None else spread + term
    return q + spread


def weight(k, other, speed, up, inside=None):
    a = (0.5 * time_step) * (k + other)
    b = (-time_step) * jnp.minimum(speed, 0.0) if up else time_step * jnp.maximum(speed, 0.0)
    if inside is not None:
        a, b = jnp.where(inside, a, 0.0), jnp.where(inside, b, 0.0)
    return a, b


def weights_x(k, k_behind, k_ahead, u, store):
    for n, other in enumerate((k_behind, k_ahead)):
        store(n, *weight(k, other, u, n == 1))


def weights_yz(k, v, w, store):
    lane = lax.broadcasted_iota(jnp.int32, k.shape, k.ndim - 1)
    y, z = lane // SIDE, lane % SIDE
    sides = ((-SIDE, v, y > 0), (SIDE, v, y < SIDE - 1), (-1, w, z > 0), (1, w, z < SIDE - 1))
    for n, (shift, speed, inside) in enumerate(sides):
        store(2 + n, *weight(k, moved(k, shift), speed, shift > 0, inside))


def joined(q, first, last):
    rows = q.shape[0]
    row = lax.broadcasted_iota(jnp.int32, q.shape, 0)
    behind = jnp.where(row == 0, jnp.broadcast_to(first, q.shape), pltpu.roll(q, 1, 0))
    ahead = jnp.where(row == rows - 1, jnp.broadcast_to(last, q.shape), pltpu.roll(q, rows - 1, 0))
    return behind, ahead


I32 = jnp.int32
CAPS = (6, 5, 10, 7)
LAGS = (0, 2, 4, 6, 8)
PIECES = 1
ROWS = SIDE // PIECES
RING = 4
NODES = RING * RING
TABLE = 256
FINAL = 128
NONE = 16 + 2 * sum(CAPS)


def count(mask):
    return jnp.sum(jnp.where(mask, 1, 0), axis=0, keepdims=True)


def column(row):
    n = row.shape[1]
    eye = lax.broadcasted_iota(I32, (n, n), 0) == lax.broadcasted_iota(I32, (n, n), 1)
    return jnp.sum(jnp.where(eye, row, 0), axis=1, keepdims=True)


def node_values(values, at):
    across = lax.broadcasted_iota(I32, (NODES, 128), 0) == lax.broadcasted_iota(I32, (NODES, 128), 1)
    values = jnp.sum(jnp.where(across, values, 0), axis=1, keepdims=True)
    there = lax.broadcasted_iota(I32, (NODES, at.shape[1]), 0) == at
    return jnp.sum(jnp.where(there, values, 0), axis=0, keepdims=True)


def balanced(n1, n2, n3, most):
    up = lambda x: pltpu.roll(x, 128 - RING, 1)
    down = lambda x: pltpu.roll(x, RING, 1)
    place = lax.broadcasted_iota(I32, n1.shape, 1) // RING % 2
    within = lambda x: jnp.minimum(jnp.maximum(x, jnp.maximum(n2 - most, 0)), jnp.minimum(n2, most))
    half = within((n2 + n3 - n1 + 1) >> 1)
    for turn in (0, 1):
        rest = n2 - half
        with_up = jnp.maximum(n1 + down(half), up(n1) + up(half))
        with_down = jnp.maximum(n3 + up(rest), down(n3) + down(rest))
        half = jnp.where(place == turn, within((with_down + n2 - with_up + 1) >> 1), half)
    return half


def hops(at, d, first, second):
    n = at.shape[1]
    earlier = lax.broadcasted_iota(I32, (n, n), 0) < lax.broadcasted_iota(I32, (n, n), 1)
    at_c, d_c = column(at), column(d)
    r = count((at_c == at) & (d_c == d) & earlier)
    here = at_c == lax.broadcasted_iota(I32, (n, 128), 1) % NODES
    n1, n2, n3 = (count(here & (d_c == k)) for k in (1, 2, 3))
    half = balanced(n1, n2, n3, min(first, second))
    node_up, node_down = (at + RING) % NODES, (at + NODES - RING) % NODES
    ups, downs = node_values(half, at), node_values(n2 - half, at)
    two = d == 2
    up = jnp.where(two, jnp.where(r < ups, 1, 0), jnp.where(d == 1, 1, 0))
    rank = jnp.where(two, jnp.where(r < ups, r, r - ups), jnp.where(d == 1, ups + r, downs + r))
    mid = jnp.where(up == 1, node_up, node_down)
    local = jnp.where(up == 1, node_values(n1 + half, node_up), node_values(n3 + n2 - half, node_down))
    late = rank >= first
    slot = jnp.where(two, jnp.maximum(local - first, 0) + rank, rank - first)
    lost = (two & (late | (slot >= second))) | ((d > 0) & jnp.logical_not(two) & (slot >= second))
    return up, rank, late, slot, mid, jnp.sum(jnp.where(lost, 1, 0), keepdims=True)


def plan(owner, z, y, net):
    ka, kb, kc, kd = CAPS
    b = lax.broadcasted_iota(I32, owner.shape, 1)
    home = b // 8
    moving = owner != home

    def pq(chip):
        return (chip % RING, chip // RING) if net == 0 else (chip // RING, chip % RING)

    node = lambda p, q: p * RING + q
    p0, q0 = pq(home // 2)
    p1, q1 = pq(jnp.where(moving, owner, home) // 2)
    my_p, my_q = (y, z) if net == 0 else (z, y)
    me, me2 = node(my_p, my_q), node(my_q, my_p)
    turn = lambda p, k: (p + k) % RING
    base_a = 16
    base_b = base_a + 2 * ka
    base_c = base_b + 2 * kb
    base_d = base_c + 2 * kc
    own = b % 16
    d1 = turn(p1 - p0, RING)
    up1, rank1, late1, slot1, mid1, lost1 = hops(node(p0, q0), d1, ka, kb)
    in_a = base_a + (1 - up1) * ka + rank1
    at1 = jnp.where(d1 == 0, own, jnp.where((d1 == 2) | late1, base_b + (1 - up1) * kb + slot1, in_a))
    d2 = turn(q1 - q0, RING)
    up2, rank2, late2, slot2, mid2, lost2 = hops(node(q0, p1), d2, kc, kd)
    in_c = base_c + (1 - up2) * kc + rank2
    at2 = jnp.where(d2 == 0, at1, jnp.where((d2 == 2) | late2, base_d + (1 - up2) * kd + slot2, in_c))
    nodes = (node(p0, q0), node(q0, p1), node(q1, p1))
    entries = (
        ((nodes[0] == me) & (d1 > 0) & jnp.logical_not(late1), (1 - up1) * ka + rank1, own),
        ((nodes[0] == me) & (d1 > 0) & (d1 != 2) & late1, 2 * ka + (1 - up1) * kb + slot1, own),
        ((mid1 == me) & (d1 == 2), 2 * ka + (1 - up1) * kb + slot1, in_a),
        ((nodes[1] == me2) & (d2 > 0) & jnp.logical_not(late2), 2 * (ka + kb) + (1 - up2) * kc + rank2, at1),
        ((nodes[1] == me2) & (d2 > 0) & (d2 != 2) & late2, 2 * (ka + kb + kc) + (1 - up2) * kd + slot2, at1),
        ((mid2 == me2) & (d2 == 2), 2 * (ka + kb + kc) + (1 - up2) * kd + slot2, in_c),
        ((nodes[2] == me2) & moving, FINAL + (owner % 2) * 32 + home, at2 - NONE),
    )
    return [(jnp.where(mask, slot, -1), place) for mask, slot, place in entries], lost1 + lost2


def both_plans(owner, z, y, core):
    n = owner.shape[1]
    one, lost_one = plan(owner, z, y, 0)
    two, lost_two = plan(owner, z, y, 1)
    number = lax.broadcasted_iota(I32, (TABLE, n), 0)
    table = jnp.zeros((TABLE, n), I32)
    for (slot_one, place_one), (slot_two, place_two) in zip(one, two):
        slot, place = jnp.where(core == 0, slot_one, slot_two), jnp.where(core == 0, place_one, place_two)
        table = table + jnp.where(number == slot, place, 0)
    table = jnp.sum(table, axis=1, keepdims=True)
    eye = lax.broadcasted_iota(I32, (TABLE, TABLE), 0) == lax.broadcasted_iota(I32, (TABLE, TABLE), 1)
    row = jnp.sum(jnp.where(eye, table, 0), axis=0, keepdims=True)
    lane = lax.broadcasted_iota(I32, row.shape, 1)
    row = jnp.clip(row + jnp.where(lane >= FINAL, NONE, 0), 0, NONE)
    return jnp.where(lane == TABLE - 1, jnp.broadcast_to(jnp.minimum(lost_one + lost_two, 1), row.shape), row)


def regrid_kernel(
    fields, boxes, homes, owner_row, owner_hbm, scale_hbm, state_hbm, kappa_hbm, flow_hbm, out, res_hbm, lost,
    res, state, kappa, flow, up, down, low, high, wm, we, edge, sib, pool, fin, sa, sb, sc, sd, ra, rb, rc, rd,
    row, table, owner, scale, in_sem, halo_sem, halo_sent, sib_sem, sib_sent, fin_sem, keep_sem, send, recv,
):
    xs, bx, n_xs = lax.axis_index("xs"), lax.axis_index("bx"), lax.axis_size("xs")
    chip, core = bx // 2, bx % 2
    z, y = chip // RING, chip % RING
    half = fields // 2

    def device(dz, dy):
        return (xs, (((z + dz) % RING) * RING + (y + dy) % RING) * 2 + core)

    def peer(ring, step):
        along_y = (1 - core) if ring == 0 else core
        return device(step * (1 - along_y), step * along_y)

    sibling = (xs, bx + 1 - 2 * core)
    after, before = (lax.rem(xs + 1, n_xs), bx), (lax.rem(xs + n_xs - 1, n_xs), bx)
    around = [peer(ring, step) for ring in (0, 1) for step in (1, RING - 1)]
    barrier = pltpu.get_barrier_semaphore()
    for other in (after, before, sibling, *around):
        pl.semaphore_signal(barrier, inc=1, device_id=other, device_id_type=MESH)
    loads = [
        pltpu.make_async_copy(src, dst, in_sem.at[i])
        for i, (src, dst) in enumerate(
            ((state_hbm, state), (kappa_hbm, kappa), (flow_hbm, flow), (owner_hbm, owner), (scale_hbm, scale))
        )
    ]
    for copy in loads:
        copy.start()
    for copy in loads:
        copy.wait()

    far_k, near_k, near_v = 2 * fields, 2 * fields + 1, 2 * fields + 2
    for buf, far, near in ((up, SIDE - 2, SIDE - 1), (down, 1, 0)):
        for b in range(boxes):
            one = pl.ds(b, 1)
            buf[far_k, one, :] = kappa[b, pl.ds(far, 1), :]
            buf[near_k, one, :] = kappa[b, pl.ds(near, 1), :]
            for d in range(3):
                buf[near_v + d, one, :] = flow[b, d, pl.ds(near, 1), :]

        @pl.loop(0, half)
        def _(t, buf=buf, far=far, near=near):
            for i in (0, 1):
                for side, row in enumerate((far, near)):
                    rows = [state[b, i * half + t, pl.ds(row, 1), :] for b in range(boxes)]
                    for b in range(boxes):
                        buf[4 * t + 2 * i + side, pl.ds(b, 1), :] = rows[b]

    pl.semaphore_wait(barrier, 3 + len(around))

    def ends_of(way, first, rows, part):
        src, dst, other = ((up, low, after), (down, high, before))[way]
        return pltpu.make_async_remote_copy(
            src_ref=src.at[pl.ds(first, rows)],
            dst_ref=dst.at[pl.ds(first, rows)],
            send_sem=halo_sent.at[way],
            recv_sem=halo_sem.at[way, part],
            device_id=other,
            device_id_type=MESH,
        )

    coefficients = [ends_of(way, far_k, 5, half) for way in (0, 1)]
    for copy in coefficients:
        copy.start()

    def send_ends(t):
        for way in (0, 1):
            ends_of(way, 4 * t, 4, t).start()

    send_ends(0)
    send_ends(1)
    def keep(ref, at):
        def store(n, a, b):
            ref[(0, n) + at] = a
            ref[(1, n) + at] = b

        return store

    row[...] = both_plans(owner_row[...], z, y, core)
    to_scalars = pltpu.make_async_copy(row, table, in_sem.at[5])
    to_scalars.start()
    for b in range(boxes):
        weights_yz(kappa[b], flow[b, 1], flow[b, 2], keep(wm, (b,)))
    for copy in coefficients:
        copy.wait_recv()

    @pl.loop(2, half)
    def _(t):
        send_ends(t)

    for i, (halo, own) in enumerate(((low, down), (high, up))):
        k, ends = halo[near_k], (halo[far_k], own[near_k])
        weights_x(k, *(ends if i == 0 else ends[::-1]), halo[near_v], keep(we, (i,)))
        weights_yz(k, halo[near_v + 1], halo[near_v + 2], keep(we, (i,)))
    for b in range(boxes):
        k = kappa[b]
        behind, ahead = joined(k, low[near_k, pl.ds(b, 1), :], high[near_k, pl.ds(b, 1), :])
        weights_x(k, behind, ahead, flow[b, 0], keep(wm, (b,)))

    def advance(t, k):
        f = k * half + t
        s = scale[f]
        far, near = 4 * t + 2 * k, 4 * t + 2 * k + 1
        for i, (halo, own) in enumerate(((low, down), (high, up))):
            ends = (halo[far], own[near])
            edge[i] = update(halo[near], *(ends if i == 0 else ends[::-1]), lambda n: (we[0, n, i], we[1, n, i]), s)
        for b in range(boxes):
            load = lambda n: (wm[0, n, b], wm[1, n, b])
            one = pl.ds(b, 1)
            q = state[b, f]
            q = update(q, *joined(q, low[near, one, :], high[near, one, :]), load, s)
            q = update(q, *joined(q, edge[0, one, :], edge[1, one, :]), load, s)
            res[f, b] = q
            out[b, k, t] = jnp.where(owner[bx * boxes + b] == bx, q, 0.0)

    def to_sibling(src, dst, t):
        return pltpu.make_async_remote_copy(
            src_ref=src, dst_ref=dst, send_sem=sib_sent.at[0], recv_sem=sib_sem.at[t], device_id=sibling, device_id_type=MESH
        )

    def rows_of(part):
        return part // PIECES, pl.ds(pl.multiple_of(part % PIECES * ROWS, ROWS), ROWS)

    def share(part):
        t, rows = rows_of(part)
        return to_sibling(res.at[(1 - core) * half + t, :, rows], sib.at[part], part)

    def back(src, dst):
        return pltpu.make_async_remote_copy(
            src_ref=src, dst_ref=dst, send_sem=fin_sem.at[0], recv_sem=fin_sem.at[1], device_id=sibling, device_id_type=MESH
        )

    def kept(k, t):
        return pltpu.make_async_copy(res.at[k * half + t], res_hbm.at[:, k * half + t], keep_sem.at[k, t])

    outgoing, incoming = (sa, sb, sc, sd), (ra, rb, rc, rd)
    start = [2 * sum(CAPS[:i]) for i in range(4)]

    def hop(stage, way, t):
        return pltpu.make_async_remote_copy(
            src_ref=outgoing[stage].at[t, way],
            dst_ref=incoming[stage].at[t, way],
            send_sem=send.at[stage],
            recv_sem=recv.at[stage, way, t],
            device_id=around[(stage // 2) * 2 + way],
            device_id_type=MESH,
        )

    def compute(t):
        for way in (0, 1):
            ends_of(way, 4 * t, 4, t).wait_recv()

        @pl.loop(0, 2)
        def _(k):
            advance(t, k)

        for piece in range(PIECES):
            share(t * PIECES + piece).start()
        kept(0, t).start()
        kept(1, t).start()

    def pick(t, first, places, store):
        for k in range(0, places, 6 * PIECES):
            group = range(k, min(k + 6 * PIECES, places))
            values = [pool[t, table[0, first + j]] for j in group]
            for j, value in zip(group, values):
                store(j, value)

    def gather(stage, t):
        slots = CAPS[stage]
        for way in (0, 1):

            def store(k, value, way=way):
                outgoing[stage][t, way, k] = value

            pick(t, start[stage] + way * slots, slots, store)
            hop(stage, way, t).start()

    def take(stage, t):
        for way in (0, 1):
            hop(stage, way, t).wait_recv()
            pool[t, pl.ds(16 + start[stage] + way * CAPS[stage], CAPS[stage])] = incoming[stage][t, way]

    def first(part):
        share(part).wait_recv()
        t, rows = rows_of(part)
        pool[part, pl.ds(core * boxes, boxes)] = res[core * half + t, :, rows]
        pool[part, pl.ds((1 - core) * boxes, boxes)] = sib[part]
        pool[part, NONE] = jnp.zeros((ROWS, LANES), jnp.float32)
        gather(0, part)

    def middle(stage):
        def run(t):
            take(stage - 1, t)
            gather(stage, t)

        return run

    def last(part):
        take(3, part)
        t, rows = rows_of(part)

        def store_far(h, value):
            fin[part, h] = value

        def store_near(h, value):
            out[boxes + h, core, t, rows] = value

        pick(part, FINAL + (1 - core) * 32, homes, store_far)
        back(fin.at[part], out.at[pl.ds(boxes, homes), core, t, rows]).start()
        pick(part, FINAL + core * 32, homes, store_near)

    steps = (first, middle(1), middle(2), middle(3), last)
    compute(0)
    compute(1)
    to_scalars.wait()
    lost[0] = table[0, TABLE - 1]

    parts = half * PIECES

    @pl.loop(0, parts + LAGS[-1])
    def _(t):
        for lag, run in zip(LAGS, steps):

            @pl.when((t >= lag) & (t < parts + lag))
            def _(run=run, lag=lag):
                run(t - lag)

            if lag == 0:

                @pl.when((t % PIECES == 0) & (t // PIECES + 2 < half))
                def _():
                    compute(t // PIECES + 2)

    for way, (src, other) in enumerate(((up, after), (down, before))):
        pltpu.make_async_remote_copy(
            src_ref=src,
            dst_ref=src,
            send_sem=halo_sent.at[way],
            recv_sem=halo_sem.at[way, 0],
            device_id=other,
            device_id_type=MESH,
        ).wait_send()
    to_sibling(sib, sib, 0).wait_send()
    back(fin, fin).wait()
    for stage in range(4):
        pltpu.make_async_remote_copy(
            src_ref=outgoing[stage],
            dst_ref=incoming[stage],
            send_sem=send.at[stage],
            recv_sem=recv.at[stage, 0, 0],
            device_id=sibling,
            device_id_type=MESH,
        ).wait_send()

    @pl.loop(0, half)
    def _(t):
        for k in (0, 1):
            kept(k, t).wait()


def regrid(owner_row, new_owner, scale, state, kappa, flow):
    boxes, fields = state.shape[:2]
    homes = new_owner.shape[0] // boxes
    half = fields // 2
    f32 = jnp.float32
    vmem, smem, hbm = (pl.BlockSpec(memory_space=m) for m in (pltpu.VMEM, pltpu.SMEM, pltpu.HBM))
    box = (SIDE, LANES)
    halo = pltpu.VMEM((2 * fields + 5, boxes, LANES), f32)
    parts, piece = half * PIECES, (ROWS, LANES)
    slots = [pltpu.VMEM((parts, 2, k) + piece, f32) for k in CAPS]
    dma = pltpu.SemaphoreType.DMA
    return pl.pallas_call(
        functools.partial(regrid_kernel, fields, boxes, homes),
        out_shape=[
            pltpu.VMEM((boxes + homes, 2, half) + box, f32),
            pltpu.HBM((boxes, fields) + box, f32),
            jax.ShapeDtypeStruct((1,), I32),
        ],
        in_specs=[vmem, hbm, hbm, hbm, hbm, hbm],
        out_specs=[vmem, hbm, smem],
        scratch_shapes=[
            pltpu.VMEM((fields, boxes) + box, f32),
            pltpu.VMEM((boxes, fields) + box, f32),
            pltpu.VMEM((boxes,) + box, f32),
            pltpu.VMEM((boxes, 3) + box, f32),
            halo,
            halo,
            halo,
            halo,
            pltpu.VMEM((2, 6, boxes) + box, f32),
            pltpu.VMEM((2, 6, 2, boxes, LANES), f32),
            pltpu.VMEM((2, boxes, LANES), f32),
            pltpu.VMEM((parts, boxes) + piece, f32),
            pltpu.VMEM((parts, NONE + 1) + piece, f32),
            pltpu.VMEM((parts, homes) + piece, f32),
            *slots,
            *slots,
            pltpu.VMEM((1, TABLE), I32),
            pltpu.SMEM((1, TABLE), I32),
            pltpu.SMEM(new_owner.shape, I32),
            pltpu.SMEM(scale.shape, f32),
            dma((6,)),
            dma((2, half + 1)),
            dma((2,)),
            dma((parts,)),
            dma((1,)),
            dma((2,)),
            dma((2, half)),
            dma((4,)),
            dma((4, 2, parts)),
        ],
        compiler_params=pltpu.CompilerParams(collective_id=0, has_side_effects=True, vmem_limit_bytes=38 << 20),
        name="regrid",
    )(owner_row, new_owner, scale, state, kappa, flow)


def place_kernel(held, out, sem):
    parts = sem.shape[0]
    rows = held.shape[0] // parts
    copies = [
        pltpu.make_async_copy(held.at[pl.ds(i * rows, rows)], out.at[pl.ds(i * rows, rows)], sem.at[i])
        for i in range(parts)
    ]
    for copy in copies:
        copy.start()
    for copy in copies:
        copy.wait()


def placed(held):
    return pl.pallas_call(
        place_kernel,
        out_shape=pltpu.HBM(held.shape, held.dtype),
        in_specs=[pl.BlockSpec(memory_space=pltpu.VMEM)],
        out_specs=pl.BlockSpec(memory_space=pltpu.HBM),
        scratch_shapes=[pltpu.SemaphoreType.DMA((8,))],
        compiler_params=pltpu.CompilerParams(vmem_limit_bytes=12 << 20),
        name="placed",
    )(held)


def dense(result, new_owner):
    owners, here = lax.axis_size("bx"), lax.axis_index("bx")
    holding = result.shape[0]
    local_owner = lax.dynamic_slice_in_dim(new_owner, here * holding, holding)
    moving = local_owner != here
    targets = jnp.arange(owners, dtype=I32)
    picked = (local_owner[None, :] == targets[:, None]) & moving[None, :]
    source = jnp.sum(jnp.where(picked, jnp.arange(holding, dtype=I32)[None, :], 0), axis=1)
    present = jnp.any(picked, axis=1).reshape(owners, 1, 1, 1)
    chosen = result[:1]
    for b in range(1, holding):
        chosen = jnp.where((source == b).reshape(owners, 1, 1, 1), result[b], chosen)
    arrived = lax.all_to_all(jnp.where(present, chosen, 0.0), "bx", split_axis=0, concat_axis=0, tiled=True)
    staying = jnp.logical_not(moving).reshape(holding, 1, 1, 1)
    return jnp.concatenate([jnp.where(staying, result, 0.0), arrived], axis=0)


def on_device(state, diffusivity, velocity, species_scale, new_owner):
    inputs = (
        pltpu.with_memory_space_constraint(x, pltpu.HBM)
        for x in (new_owner, species_scale, state[0], diffusivity[0], velocity[0])
    )
    held, res, lost = regrid(new_owner.reshape(1, -1), *inputs)
    out = placed(held).reshape((held.shape[0],) + state.shape[2:])

    def again(i, out):
        _, owner = lax.optimization_barrier((i, new_owner))
        return dense(res, owner)

    return lax.fori_loop(0, lost[0], again, out)[None]


def solution(mesh):
    in_specs = (
        P("xs", "bx", None, None, None),
        P("xs", "bx", None, None),
        P("xs", "bx", None, None, None),
        P(),
        P(),
    )
    out_specs = P("xs", "bx", None, None, None)
    return jax.shard_map(on_device, mesh=mesh, in_specs=in_specs, out_specs=out_specs, check_vma=False)
```

```python
import functools

import jax
import jax.numpy as jnp
from jax import lax
from jax.experimental import pallas as pl
from jax.experimental.pallas import tpu as pltpu
from jax.sharding import PartitionSpec as P

MESH = pl.DeviceIdType.MESH
time_step = 0.03
SIDE = 16
LANES = SIDE * SIDE


def moved(q, shift):
    return pltpu.roll(q, (-shift) % LANES, q.ndim - 1)


def update(q, behind, ahead, load, s):
    spread = None
    for n, other in enumerate(
        (behind, ahead, moved(q, -SIDE), moved(q, SIDE), moved(q, -1), moved(q, 1))
    ):
        a, b = load(n)
        term = (s * a + b) * (other - q)
        spread = term if spread is None else spread + term
    return q + spread


def weight(k, other, speed, up, inside=None):
    a = (0.5 * time_step) * (k + other)
    b = (-time_step) * jnp.minimum(speed, 0.0) if up else time_step * jnp.maximum(speed, 0.0)
    if inside is not None:
        a, b = jnp.where(inside, a, 0.0), jnp.where(inside, b, 0.0)
    return a, b


def weights_x(k, k_behind, k_ahead, u, store):
    for n, other in enumerate((k_behind, k_ahead)):
        store(n, *weight(k, other, u, n == 1))


def weights_yz(k, v, w, store):
    lane = lax.broadcasted_iota(jnp.int32, k.shape, k.ndim - 1)
    y, z = lane // SIDE, lane % SIDE
    sides = ((-SIDE, v, y > 0), (SIDE, v, y < SIDE - 1), (-1, w, z > 0), (1, w, z < SIDE - 1))
    for n, (shift, speed, inside) in enumerate(sides):
        store(2 + n, *weight(k, moved(k, shift), speed, shift > 0, inside))


def joined(q, first, last):
    rows = q.shape[0]
    row = lax.broadcasted_iota(jnp.int32, q.shape, 0)
    behind = jnp.where(row == 0, jnp.broadcast_to(first, q.shape), pltpu.roll(q, 1, 0))
    ahead = jnp.where(row == rows - 1, jnp.broadcast_to(last, q.shape), pltpu.roll(q, rows - 1, 0))
    return behind, ahead


I32 = jnp.int32
CAPS = (6, 5, 10, 7)
LAGS = (0, 2, 4, 6, 8)
PIECES = 1
ROWS = SIDE // PIECES
RING = 4
NODES = RING * RING
TABLE = 256
FINAL = 128
NONE = 16 + 2 * sum(CAPS)


def count(mask):
    return jnp.sum(jnp.where(mask, 1, 0), axis=0, keepdims=True)


def column(row):
    n = row.shape[1]
    eye = lax.broadcasted_iota(I32, (n, n), 0) == lax.broadcasted_iota(I32, (n, n), 1)
    return jnp.sum(jnp.where(eye, row, 0), axis=1, keepdims=True)


def node_values(values, at):
    across = lax.broadcasted_iota(I32, (NODES, 128), 0) == lax.broadcasted_iota(I32, (NODES, 128), 1)
    values = jnp.sum(jnp.where(across, values, 0), axis=1, keepdims=True)
    there = lax.broadcasted_iota(I32, (NODES, at.shape[1]), 0) == at
    return jnp.sum(jnp.where(there, values, 0), axis=0, keepdims=True)


def balanced(n1, n2, n3, most):
    up = lambda x: pltpu.roll(x, 128 - RING, 1)
    down = lambda x: pltpu.roll(x, RING, 1)
    place = lax.broadcasted_iota(I32, n1.shape, 1) // RING % 2
    within = lambda x: jnp.minimum(jnp.maximum(x, jnp.maximum(n2 - most, 0)), jnp.minimum(n2, most))
    half = within((n2 + n3 - n1 + 1) >> 1)
    for turn in (0, 1):
        rest = n2 - half
        with_up = jnp.maximum(n1 + down(half), up(n1) + up(half))
        with_down = jnp.maximum(n3 + up(rest), down(n3) + down(rest))
        half = jnp.where(place == turn, within((with_down + n2 - with_up + 1) >> 1), half)
    return half


def hops(at, d, first, second):
    n = at.shape[1]
    earlier = lax.broadcasted_iota(I32, (n, n), 0) < lax.broadcasted_iota(I32, (n, n), 1)
    at_c, d_c = column(at), column(d)
    r = count((at_c == at) & (d_c == d) & earlier)
    here = at_c == lax.broadcasted_iota(I32, (n, 128), 1) % NODES
    n1, n2, n3 = (count(here & (d_c == k)) for k in (1, 2, 3))
    half = balanced(n1, n2, n3, min(first, second))
    node_up, node_down = (at + RING) % NODES, (at + NODES - RING) % NODES
    ups, downs = node_values(half, at), node_values(n2 - half, at)
    two = d == 2
    up = jnp.where(two, jnp.where(r < ups, 1, 0), jnp.where(d == 1, 1, 0))
    rank = jnp.where(two, jnp.where(r < ups, r, r - ups), jnp.where(d == 1, ups + r, downs + r))
    mid = jnp.where(up == 1, node_up, node_down)
    local = jnp.where(up == 1, node_values(n1 + half, node_up), node_values(n3 + n2 - half, node_down))
    late = rank >= first
    slot = jnp.where(two, jnp.maximum(local - first, 0) + rank, rank - first)
    lost = (two & (late | (slot >= second))) | ((d > 0) & jnp.logical_not(two) & (slot >= second))
    return up, rank, late, slot, mid, jnp.sum(jnp.where(lost, 1, 0), keepdims=True)


def plan(owner, z, y, net):
    ka, kb, kc, kd = CAPS
    b = lax.broadcasted_iota(I32, owner.shape, 1)
    home = b // 8
    moving = owner != home

    def pq(chip):
        return (chip % RING, chip // RING) if net == 0 else (chip // RING, chip % RING)

    node = lambda p, q: p * RING + q
    p0, q0 = pq(home // 2)
    p1, q1 = pq(jnp.where(moving, owner, home) // 2)
    my_p, my_q = (y, z) if net == 0 else (z, y)
    me, me2 = node(my_p, my_q), node(my_q, my_p)
    turn = lambda p, k: (p + k) % RING
    base_a = 16
    base_b = base_a + 2 * ka
    base_c = base_b + 2 * kb
    base_d = base_c + 2 * kc
    own = b % 16
    d1 = turn(p1 - p0, RING)
    up1, rank1, late1, slot1, mid1, lost1 = hops(node(p0, q0), d1, ka, kb)
    in_a = base_a + (1 - up1) * ka + rank1
    at1 = jnp.where(d1 == 0, own, jnp.where((d1 == 2) | late1, base_b + (1 - up1) * kb + slot1, in_a))
    d2 = turn(q1 - q0, RING)
    up2, rank2, late2, slot2, mid2, lost2 = hops(node(q0, p1), d2, kc, kd)
    in_c = base_c + (1 - up2) * kc + rank2
    at2 = jnp.where(d2 == 0, at1, jnp.where((d2 == 2) | late2, base_d + (1 - up2) * kd + slot2, in_c))
    nodes = (node(p0, q0), node(q0, p1), node(q1, p1))
    entries = (
        ((nodes[0] == me) & (d1 > 0) & jnp.logical_not(late1), (1 - up1) * ka + rank1, own),
        ((nodes[0] == me) & (d1 > 0) & (d1 != 2) & late1, 2 * ka + (1 - up1) * kb + slot1, own),
        ((mid1 == me) & (d1 == 2), 2 * ka + (1 - up1) * kb + slot1, in_a),
        ((nodes[1] == me2) & (d2 > 0) & jnp.logical_not(late2), 2 * (ka + kb) + (1 - up2) * kc + rank2, at1),
        ((nodes[1] == me2) & (d2 > 0) & (d2 != 2) & late2, 2 * (ka + kb + kc) + (1 - up2) * kd + slot2, at1),
        ((mid2 == me2) & (d2 == 2), 2 * (ka + kb + kc) + (1 - up2) * kd + slot2, in_c),
        ((nodes[2] == me2) & moving, FINAL + (owner % 2) * 32 + home, at2 - NONE),
    )
    return [(jnp.where(mask, slot, -1), place) for mask, slot, place in entries], lost1 + lost2


def both_plans(owner, z, y, core):
    n = owner.shape[1]
    one, lost_one = plan(owner, z, y, 0)
    two, lost_two = plan(owner, z, y, 1)
    number = lax.broadcasted_iota(I32, (TABLE, n), 0)
    table = jnp.zeros((TABLE, n), I32)
    for (slot_one, place_one), (slot_two, place_two) in zip(one, two):
        slot, place = jnp.where(core == 0, slot_one, slot_two), jnp.where(core == 0, place_one, place_two)
        table = table + jnp.where(number == slot, place, 0)
    table = jnp.sum(table, axis=1, keepdims=True)
    eye = lax.broadcasted_iota(I32, (TABLE, TABLE), 0) == lax.broadcasted_iota(I32, (TABLE, TABLE), 1)
    row = jnp.sum(jnp.where(eye, table, 0), axis=0, keepdims=True)
    lane = lax.broadcasted_iota(I32, row.shape, 1)
    row = jnp.clip(row + jnp.where(lane >= FINAL, NONE, 0), 0, NONE)
    return jnp.where(lane == TABLE - 1, jnp.broadcast_to(jnp.minimum(lost_one + lost_two, 1), row.shape), row)


def regrid_kernel(
    fields, boxes, homes, owner_row, owner_hbm, scale_hbm, state_hbm, kappa_hbm, flow_hbm, out, res_hbm, lost,
    res, state, kappa, flow, up, down, low, high, wm, we, edge, sib, pool, fin, sa, sb, sc, sd, ra, rb, rc, rd,
    row, table, owner, scale, in_sem, halo_sem, halo_sent, sib_sem, sib_sent, fin_sem, keep_sem, send, recv,
):
    xs, bx, n_xs = lax.axis_index("xs"), lax.axis_index("bx"), lax.axis_size("xs")
    chip, core = bx // 2, bx % 2
    z, y = chip // RING, chip % RING
    half = fields // 2

    def device(dz, dy):
        return (xs, (((z + dz) % RING) * RING + (y + dy) % RING) * 2 + core)

    def peer(ring, step):
        along_y = (1 - core) if ring == 0 else core
        return device(step * (1 - along_y), step * along_y)

    sibling = (xs, bx + 1 - 2 * core)
    after, before = (lax.rem(xs + 1, n_xs), bx), (lax.rem(xs + n_xs - 1, n_xs), bx)
    around = [peer(ring, step) for ring in (0, 1) for step in (1, RING - 1)]
    barrier = pltpu.get_barrier_semaphore()
    for other in (after, before, sibling, *around):
        pl.semaphore_signal(barrier, inc=1, device_id=other, device_id_type=MESH)
    loads = [
        pltpu.make_async_copy(src, dst, in_sem.at[i])
        for i, (src, dst) in enumerate(
            ((state_hbm, state), (kappa_hbm, kappa), (flow_hbm, flow), (owner_hbm, owner), (scale_hbm, scale))
        )
    ]
    for copy in loads:
        copy.start()
    for copy in loads:
        copy.wait()

    far_k, near_k, near_v = 2 * fields, 2 * fields + 1, 2 * fields + 2
    for buf, far, near in ((up, SIDE - 2, SIDE - 1), (down, 1, 0)):
        for b in range(boxes):
            one = pl.ds(b, 1)
            buf[far_k, one, :] = kappa[b, pl.ds(far, 1), :]
            buf[near_k, one, :] = kappa[b, pl.ds(near, 1), :]
            for d in range(3):
                buf[near_v + d, one, :] = flow[b, d, pl.ds(near, 1), :]

        @pl.loop(0, half)
        def _(t, buf=buf, far=far, near=near):
            for i in (0, 1):
                for side, row in enumerate((far, near)):
                    rows = [state[b, i * half + t, pl.ds(row, 1), :] for b in range(boxes)]
                    for b in range(boxes):
                        buf[4 * t + 2 * i + side, pl.ds(b, 1), :] = rows[b]

    pl.semaphore_wait(barrier, 3 + len(around))

    def ends_of(way, first, rows, part):
        src, dst, other = ((up, low, after), (down, high, before))[way]
        return pltpu.make_async_remote_copy(
            src_ref=src.at[pl.ds(first, rows)],
            dst_ref=dst.at[pl.ds(first, rows)],
            send_sem=halo_sent.at[way],
            recv_sem=halo_sem.at[way, part],
            device_id=other,
            device_id_type=MESH,
        )

    coefficients = [ends_of(way, far_k, 5, half) for way in (0, 1)]
    for copy in coefficients:
        copy.start()

    def send_ends(t):
        for way in (0, 1):
            ends_of(way, 4 * t, 4, t).start()

    send_ends(0)
    send_ends(1)
    def keep(ref, at):
        def store(n, a, b):
            ref[(0, n) + at] = a
            ref[(1, n) + at] = b

        return store

    row[...] = both_plans(owner_row[...], z, y, core)
    to_scalars = pltpu.make_async_copy(row, table, in_sem.at[5])
    to_scalars.start()
    for b in range(boxes):
        weights_yz(kappa[b], flow[b, 1], flow[b, 2], keep(wm, (b,)))
    for copy in coefficients:
        copy.wait_recv()

    @pl.loop(2, half)
    def _(t):
        send_ends(t)

    for i, (halo, own) in enumerate(((low, down), (high, up))):
        k, ends = halo[near_k], (halo[far_k], own[near_k])
        weights_x(k, *(ends if i == 0 else ends[::-1]), halo[near_v], keep(we, (i,)))
        weights_yz(k, halo[near_v + 1], halo[near_v + 2], keep(we, (i,)))
    for b in range(boxes):
        k = kappa[b]
        behind, ahead = joined(k, low[near_k, pl.ds(b, 1), :], high[near_k, pl.ds(b, 1), :])
        weights_x(k, behind, ahead, flow[b, 0], keep(wm, (b,)))

    def advance(t, k):
        f = k * half + t
        s = scale[f]
        far, near = 4 * t + 2 * k, 4 * t + 2 * k + 1
        for i, (halo, own) in enumerate(((low, down), (high, up))):
            ends = (halo[far], own[near])
            edge[i] = update(halo[near], *(ends if i == 0 else ends[::-1]), lambda n: (we[0, n, i], we[1, n, i]), s)
        for b in range(boxes):
            load = lambda n: (wm[0, n, b], wm[1, n, b])
            one = pl.ds(b, 1)
            q = state[b, f]
            q = update(q, *joined(q, low[near, one, :], high[near, one, :]), load, s)
            q = update(q, *joined(q, edge[0, one, :], edge[1, one, :]), load, s)
            res[f, b] = q
            out[b, k, t] = jnp.where(owner[bx * boxes + b] == bx, q, 0.0)

    def to_sibling(src, dst, t):
        return pltpu.make_async_remote_copy(
            src_ref=src, dst_ref=dst, send_sem=sib_sent.at[0], recv_sem=sib_sem.at[t], device_id=sibling, device_id_type=MESH
        )

    def rows_of(part):
        return part // PIECES, pl.ds(pl.multiple_of(part % PIECES * ROWS, ROWS), ROWS)

    def share(part):
        t, rows = rows_of(part)
        return to_sibling(res.at[(1 - core) * half + t, :, rows], sib.at[part], part)

    def back(src, dst):
        return pltpu.make_async_remote_copy(
            src_ref=src, dst_ref=dst, send_sem=fin_sem.at[0], recv_sem=fin_sem.at[1], device_id=sibling, device_id_type=MESH
        )

    def kept(k, t):
        return pltpu.make_async_copy(res.at[k * half + t], res_hbm.at[:, k * half + t], keep_sem.at[k, t])

    outgoing, incoming = (sa, sb, sc, sd), (ra, rb, rc, rd)
    start = [2 * sum(CAPS[:i]) for i in range(4)]

    def hop(stage, way, t):
        return pltpu.make_async_remote_copy(
            src_ref=outgoing[stage].at[t, way],
            dst_ref=incoming[stage].at[t, way],
            send_sem=send.at[stage],
            recv_sem=recv.at[stage, way, t],
            device_id=around[(stage // 2) * 2 + way],
            device_id_type=MESH,
        )

    def compute(t):
        for way in (0, 1):
            ends_of(way, 4 * t, 4, t).wait_recv()

        @pl.loop(0, 2)
        def _(k):
            advance(t, k)

        for piece in range(PIECES):
            share(t * PIECES + piece).start()
        kept(0, t).start()
        kept(1, t).start()

    def pick(t, first, places, store):
        for k in range(0, places, 6 * PIECES):
            group = range(k, min(k + 6 * PIECES, places))
            values = [pool[t, table[0, first + j]] for j in group]
            for j, value in zip(group, values):
                store(j, value)

    def gather(stage, t):
        slots = CAPS[stage]
        for way in (0, 1):

            def store(k, value, way=way):
                outgoing[stage][t, way, k] = value

            pick(t, start[stage] + way * slots, slots, store)
            hop(stage, way, t).start()

    def take(stage, t):
        for way in (0, 1):
            hop(stage, way, t).wait_recv()
            pool[t, pl.ds(16 + start[stage] + way * CAPS[stage], CAPS[stage])] = incoming[stage][t, way]

    def first(part):
        share(part).wait_recv()
        t, rows = rows_of(part)
        pool[part, pl.ds(core * boxes, boxes)] = res[core * half + t, :, rows]
        pool[part, pl.ds((1 - core) * boxes, boxes)] = sib[part]
        pool[part, NONE] = jnp.zeros((ROWS, LANES), jnp.float32)
        gather(0, part)

    def middle(stage):
        def run(t):
            take(stage - 1, t)
            gather(stage, t)

        return run

    def last(part):
        take(3, part)
        t, rows = rows_of(part)

        def store_far(h, value):
            fin[part, h] = value

        def store_near(h, value):
            out[boxes + h, core, t, rows] = value

        some = homes // 2
        for lead in (0, some):
            pick(part, FINAL + (1 - core) * 32 + lead, some, lambda h, value, lead=lead: store_far(lead + h, value))
            back(fin.at[part, pl.ds(lead, some)], out.at[pl.ds(boxes + lead, some), core, t, rows]).start()
        pick(part, FINAL + core * 32, homes, store_near)

    steps = (first, middle(1), middle(2), middle(3), last)
    compute(0)
    compute(1)
    to_scalars.wait()
    lost[0] = table[0, TABLE - 1]

    parts = half * PIECES

    @pl.loop(0, parts + LAGS[-1])
    def _(t):
        for lag, run in zip(LAGS, steps):

            @pl.when((t >= lag) & (t < parts + lag))
            def _(run=run, lag=lag):
                run(t - lag)

            if lag == 0:

                @pl.when((t % PIECES == 0) & (t // PIECES + 2 < half))
                def _():
                    compute(t // PIECES + 2)

    for way, (src, other) in enumerate(((up, after), (down, before))):
        pltpu.make_async_remote_copy(
            src_ref=src,
            dst_ref=src,
            send_sem=halo_sent.at[way],
            recv_sem=halo_sem.at[way, 0],
            device_id=other,
            device_id_type=MESH,
        ).wait_send()
    to_sibling(sib, sib, 0).wait_send()
    back(fin, fin).wait()
    for stage in range(4):
        pltpu.make_async_remote_copy(
            src_ref=outgoing[stage],
            dst_ref=incoming[stage],
            send_sem=send.at[stage],
            recv_sem=recv.at[stage, 0, 0],
            device_id=sibling,
            device_id_type=MESH,
        ).wait_send()

    @pl.loop(0, half)
    def _(t):
        for k in (0, 1):
            kept(k, t).wait()


def regrid(owner_row, new_owner, scale, state, kappa, flow):
    boxes, fields = state.shape[:2]
    homes = new_owner.shape[0] // boxes
    half = fields // 2
    f32 = jnp.float32
    vmem, smem, hbm = (pl.BlockSpec(memory_space=m) for m in (pltpu.VMEM, pltpu.SMEM, pltpu.HBM))
    box = (SIDE, LANES)
    halo = pltpu.VMEM((2 * fields + 5, boxes, LANES), f32)
    parts, piece = half * PIECES, (ROWS, LANES)
    slots = [pltpu.VMEM((parts, 2, k) + piece, f32) for k in CAPS]
    dma = pltpu.SemaphoreType.DMA
    return pl.pallas_call(
        functools.partial(regrid_kernel, fields, boxes, homes),
        out_shape=[
            pltpu.VMEM((boxes + homes, 2, half) + box, f32),
            pltpu.HBM((boxes, fields) + box, f32),
            jax.ShapeDtypeStruct((1,), I32),
        ],
        in_specs=[vmem, hbm, hbm, hbm, hbm, hbm],
        out_specs=[vmem, hbm, smem],
        scratch_shapes=[
            pltpu.VMEM((fields, boxes) + box, f32),
            pltpu.VMEM((boxes, fields) + box, f32),
            pltpu.VMEM((boxes,) + box, f32),
            pltpu.VMEM((boxes, 3) + box, f32),
            halo,
            halo,
            halo,
            halo,
            pltpu.VMEM((2, 6, boxes) + box, f32),
            pltpu.VMEM((2, 6, 2, boxes, LANES), f32),
            pltpu.VMEM((2, boxes, LANES), f32),
            pltpu.VMEM((parts, boxes) + piece, f32),
            pltpu.VMEM((parts, NONE + 1) + piece, f32),
            pltpu.VMEM((parts, homes) + piece, f32),
            *slots,
            *slots,
            pltpu.VMEM((1, TABLE), I32),
            pltpu.SMEM((1, TABLE), I32),
            pltpu.SMEM(new_owner.shape, I32),
            pltpu.SMEM(scale.shape, f32),
            dma((6,)),
            dma((2, half + 1)),
            dma((2,)),
            dma((parts,)),
            dma((1,)),
            dma((2,)),
            dma((2, half)),
            dma((4,)),
            dma((4, 2, parts)),
        ],
        compiler_params=pltpu.CompilerParams(collective_id=0, has_side_effects=True, vmem_limit_bytes=38 << 20),
        name="regrid",
    )(owner_row, new_owner, scale, state, kappa, flow)


def place_kernel(held, out, sem):
    parts = sem.shape[0]
    rows = held.shape[0] // parts
    copies = [
        pltpu.make_async_copy(held.at[pl.ds(i * rows, rows)], out.at[pl.ds(i * rows, rows)], sem.at[i])
        for i in range(parts)
    ]
    for copy in copies:
        copy.start()
    for copy in copies:
        copy.wait()


def placed(held):
    return pl.pallas_call(
        place_kernel,
        out_shape=pltpu.HBM(held.shape, held.dtype),
        in_specs=[pl.BlockSpec(memory_space=pltpu.VMEM)],
        out_specs=pl.BlockSpec(memory_space=pltpu.HBM),
        scratch_shapes=[pltpu.SemaphoreType.DMA((8,))],
        compiler_params=pltpu.CompilerParams(vmem_limit_bytes=12 << 20),
        name="placed",
    )(held)


def dense(result, new_owner):
    owners, here = lax.axis_size("bx"), lax.axis_index("bx")
    holding = result.shape[0]
    local_owner = lax.dynamic_slice_in_dim(new_owner, here * holding, holding)
    moving = local_owner != here
    targets = jnp.arange(owners, dtype=I32)
    picked = (local_owner[None, :] == targets[:, None]) & moving[None, :]
    source = jnp.sum(jnp.where(picked, jnp.arange(holding, dtype=I32)[None, :], 0), axis=1)
    present = jnp.any(picked, axis=1).reshape(owners, 1, 1, 1)
    chosen = result[:1]
    for b in range(1, holding):
        chosen = jnp.where((source == b).reshape(owners, 1, 1, 1), result[b], chosen)
    arrived = lax.all_to_all(jnp.where(present, chosen, 0.0), "bx", split_axis=0, concat_axis=0, tiled=True)
    staying = jnp.logical_not(moving).reshape(holding, 1, 1, 1)
    return jnp.concatenate([jnp.where(staying, result, 0.0), arrived], axis=0)


def on_device(state, diffusivity, velocity, species_scale, new_owner):
    inputs = (
        pltpu.with_memory_space_constraint(x, pltpu.HBM)
        for x in (new_owner, species_scale, state[0], diffusivity[0], velocity[0])
    )
    held, res, lost = regrid(new_owner.reshape(1, -1), *inputs)
    out = placed(held).reshape((held.shape[0],) + state.shape[2:])

    def again(i, out):
        _, owner = lax.optimization_barrier((i, new_owner))
        return dense(res, owner)

    return lax.fori_loop(0, lost[0], again, out)[None]


def solution(mesh):
    in_specs = (
        P("xs", "bx", None, None, None),
        P("xs", "bx", None, None),
        P("xs", "bx", None, None, None),
        P(),
        P(),
    )
    out_specs = P("xs", "bx", None, None, None)
    return jax.shard_map(on_device, mesh=mesh, in_specs=in_specs, out_specs=out_specs, check_vma=False)
```
